32 devices in a mesh: fsdp: 4 (over z), ctx: 2 (over y), tp: 4 (over x, core).
Axes of the slice: x: 2, y: 2, z: 4, core: 2. Of those that a mesh axis runs over, the one named last changes fastest.
Arguments:
- tokens: bfloat16 [1024, 768], P(('fsdp', 'ctx')), may hold values from -6 to 6
- segments: int32 [4, 256], P('fsdp'), may hold values from 0 to 3, never falling along the last dimension, each value on 1 to 128 neighbouring positions
- cotangent: float32 [1024, 768], P(('fsdp', 'ctx')), may hold values from -6 to 6
- prenorm: float32 [2, 768], replicated, may hold values from 0.5 to 1.5
- gate_proj: bfloat16 [2, 768, 1536], P(None, ('fsdp', 'ctx'), 'tp'), may hold values from -0.21875 to 0.21875
- inner_proj: bfloat16 [2, 768, 1536], P(None, ('fsdp', 'ctx'), 'tp'), may hold values from -0.21875 to 0.21875
- state_proj: bfloat16 [2, 768, 256], P(None, ('fsdp', 'ctx')), may hold values from -0.21875 to 0.21875
- step_proj: bfloat16 [2, 768, 24], P(None, ('fsdp', 'ctx'), 'tp'), may hold values from -0.21875 to 0.21875
- inner_kernel: float32 [2, 4, 1536], P(None, None, 'tp'), may hold values from -3 to 3
- inner_offset: float32 [2, 1536], P(None, 'tp'), may hold values from -3 to 3
- state_kernel: float32 [2, 4, 256], replicated, may hold values from -3 to 3
- state_offset: float32 [2, 256], replicated, may hold values from -3 to 3
- step_bias: float32 [2, 24], P(None, 'tp'), may hold values from -7 to -3
- decay_log: float32 [2, 24], P(None, 'tp'), may hold values from -3 to 1
- skip_gain: float32 [2, 24], P(None, 'tp'), may hold values from 0.5 to 1.5
- norm_gain: float32 [2, 1536], P(None, 'tp'), may hold values from 0.5 to 1.5
- mixer_out: bfloat16 [2, 768, 1536], P(None, ('fsdp', 'ctx'), 'tp'), may hold values from -0.15625 to 0.15625
Outputs:
- output: float32 [1024, 768], P(('fsdp', 'ctx'), 'tp')
- token_grad: float32 [1024, 768], P(('fsdp', 'ctx'), 'tp')
- prenorm_grad: float32 [2, 768], P(None, 'tp')
- gate_grad: float32 [2, 768, 1536], P(None, ('fsdp', 'ctx'), 'tp')
- inner_grad: float32 [2, 768, 1536], P(None, ('fsdp', 'ctx'), 'tp')
- state_grad: float32 [2, 768, 256], P(None, ('fsdp', 'ctx'))
- step_grad: float32 [2, 768, 24], P(None, ('fsdp', 'ctx'), 'tp')
- inner_kernel_grad: float32 [2, 4, 1536], P(None, None, 'tp')
- inner_offset_grad: float32 [2, 1536], P(None, 'tp')
- state_kernel_grad: float32 [2, 4, 256], replicated
- state_offset_grad: float32 [2, 256], replicated
- step_bias_grad: float32 [2, 24], P(None, 'tp')
- decay_log_grad: float32 [2, 24], P(None, 'tp')
- skip_gain_grad: float32 [2, 24], P(None, 'tp')
- norm_gain_grad: float32 [2, 1536], P(None, 'tp')
- mixer_grad: float32 [2, 768, 1536], P(None, ('fsdp', 'ctx'), 'tp')
The draws below stay inside these ranges and needn't reach their ends.
Inputs may be any that keep to these rules, and one draw needn't show every extreme that they name: `segments`: each row holds one token run; its segment numbers never fall, each sequence holds 1 to 128 tokens, and one holds exactly 128.
All inputs are finite; a program needn't handle non-finite values.
Results may differ from the reference program's by a relative error of at most 0.017.
Values may be sent and summed in bfloat16 or wider, within the bound.
A program may use at most 128 MiB of HBM per device.

```python
import math
import jax
import jax.numpy as jnp
import numpy as np
from jax import lax

D = 768
INNER = 1536
HEADS = 24
HEADDIM = 64
STATE = 128
CONV = 4
SPAN = 128
LAYERS = 2
SEQS = 4
GROUPS = 4
GROUP_TOK = 256
TOKENS = 1024
SEQ_MAX = 128


def block_scale(key, dims, shards, low, high):
    level, own = 1.0, jax.random.fold_in(key, 6)
    for dim, blocks in shards:
        heights = jnp.exp(jax.random.uniform(jax.random.fold_in(own, dim), (blocks,), jnp.float32, low / len(shards), high / len(shards)))
        level = level * jnp.repeat(heights, dims[dim] // blocks).reshape([-1 if axis == dim else 1 for axis in range(len(dims))])
    return level


def length_profile(number_of, total, most, lean):
    loads = [(1 << 20) // math.isqrt(rank ** lean) + 1 for rank in range(2, number_of + 1)]
    rest, holding = total - most - (number_of - 1), [1] * (number_of - 1)
    while rest > 0:
        free = [i for i in range(number_of - 1) if holding[i] < most]
        whole, remaining = sum([loads[i] for i in free]), rest
        for i in free:
            extra = min(most - holding[i], max(1, remaining * loads[i] // whole), rest)
            holding[i] = holding[i] + extra
            rest = rest - extra
    return np.array([most] + holding)


def ragged(stream_key, count, total, limit, slope):
    if count == 2:
        one = jax.random.randint(stream_key, (), max(1, total - limit), min(limit, total - 1) + 1)
        return jnp.stack([one, total - one])
    sizes = jnp.asarray(length_profile(count, total, limit, slope), jnp.int32)
    twos = (count - 1) // 2
    source_of, receiver = sizes[1:1 + 2 * twos:2], sizes[2:2 + 2 * twos:2]
    margin = jnp.minimum(source_of - 1, limit - receiver)
    shifted = jax.random.randint(jax.random.fold_in(stream_key, 1), (twos,), 0, 1 << 20) % (margin + 1)
    sizes = sizes.at[1:1 + 2 * twos:2].set(source_of - shifted).at[2:2 + 2 * twos:2].set(receiver + shifted)
    return sizes[jax.random.permutation(jax.random.fold_in(stream_key, 2), count)]


def normal_values(key, shape, scale, most, cuts=(), kind=jnp.bfloat16):
    level = block_scale(key, shape, cuts, -0.22, 0.18) if cuts else 1.0
    drawn = jax.random.normal(key, shape, jnp.float32) * scale * level
    return jnp.minimum(jnp.maximum(drawn, -most), most).astype(kind)


def setup_inputs(seed: int = 0) -> dict:
    streams_of = jax.random.split(jax.random.key(seed), 18)
    tokens = normal_values(streams_of[0], (TOKENS, D), 1.0, 6.0, ((0, 8),))
    segments = jax.vmap(lambda own: jnp.searchsorted(jnp.cumsum(ragged(own, SEQS, GROUP_TOK, SEQ_MAX, 2)), jnp.arange(GROUP_TOK), side="right"))(jax.random.split(streams_of[1], GROUPS)).reshape((GROUPS, GROUP_TOK)).astype(jnp.int32)
    cotangent = normal_values(streams_of[2], (TOKENS, D), 1.0, 6.0, ((0, 8),), jnp.float32)
    prenorm = jnp.clip(1.0 + 0.1 * jax.random.normal(streams_of[3], (LAYERS, D), jnp.float32), 0.5, 1.5)
    gate_proj = normal_values(streams_of[4], (LAYERS, D, INNER), D ** -0.5, 0.21875, ((1, 8), (2, 4)))
    inner_proj = normal_values(streams_of[5], (LAYERS, D, INNER), D ** -0.5, 0.21875, ((1, 8), (2, 4)))
    state_proj = normal_values(streams_of[6], (LAYERS, D, 2 * STATE), D ** -0.5, 0.21875, ((1, 8),))
    step_proj = normal_values(streams_of[7], (LAYERS, D, HEADS), D ** -0.5, 0.21875, ((1, 8), (2, 4)))
    inner_kernel = normal_values(streams_of[8], (LAYERS, CONV, INNER), 0.5, 3.0, ((2, 4),), jnp.float32)
    inner_offset = normal_values(streams_of[9], (LAYERS, INNER), 0.5, 3.0, ((1, 4),), jnp.float32)
    state_kernel = normal_values(streams_of[10], (LAYERS, CONV, 2 * STATE), 0.5, 3.0, (), jnp.float32)
    state_offset = normal_values(streams_of[11], (LAYERS, 2 * STATE), 0.5, 3.0, (), jnp.float32)
    step_bias = jnp.clip(-7.0 + 4.0 * jax.random.uniform(streams_of[12], (LAYERS, HEADS), jnp.float32) ** block_scale(streams_of[12], (LAYERS, HEADS), ((1, 4),), -0.2, 0.2), -7.0, -3.0)
    decay_log = jnp.clip(-3.0 + 4.0 * jax.random.uniform(streams_of[13], (LAYERS, HEADS), jnp.float32) ** block_scale(streams_of[13], (LAYERS, HEADS), ((1, 4),), -0.2, 0.2), -3.0, 1.0)
    skip_gain = jnp.clip(0.5 + 1.0 * jax.random.uniform(streams_of[14], (LAYERS, HEADS), jnp.float32) ** block_scale(streams_of[14], (LAYERS, HEADS), ((1, 4),), -0.2, 0.2), 0.5, 1.5)
    norm_gain = jnp.clip(1.0 + 0.1 * jax.random.normal(streams_of[15], (LAYERS, INNER), jnp.float32), 0.5, 1.5)
    mixer_out = normal_values(streams_of[16], (LAYERS, D, INNER), INNER ** -0.5, 0.15625, ((1, 8), (2, 4)))
    return {"tokens": tokens, "segments": segments, "cotangent": cotangent, "prenorm": prenorm, "gate_proj": gate_proj, "inner_proj": inner_proj, "state_proj": state_proj, "step_proj": step_proj, "inner_kernel": inner_kernel, "inner_offset": inner_offset, "state_kernel": state_kernel, "state_offset": state_offset, "step_bias": step_bias, "decay_log": decay_log, "skip_gain": skip_gain, "norm_gain": norm_gain, "mixer_out": mixer_out}


EPSILON = 1e-05
HIGH = lax.Precision.HIGHEST

def rms_apply(hidden, gain):
    inverse = lax.rsqrt(lax.optimization_barrier(jnp.mean(hidden * hidden, axis=-1, keepdims=True)) + EPSILON)
    return hidden * inverse * gain

def conv_apply(padded, seg_padded, kernel, offset):
    taps = kernel.shape[0]
    length = padded.shape[0] - taps + 1
    current = seg_padded[taps - 1:]
    total = jnp.zeros((length, padded.shape[1]), jnp.float32) + offset
    for shift_index in range(taps):
        same = (seg_padded[shift_index:shift_index + length] == current).astype(jnp.float32)
        total = total + kernel[shift_index] * padded[shift_index:shift_index + length] * same[:, None]
    return jax.nn.silu(total)

def fresh_flags(seg, cont):
    first = jnp.reshape(1.0 - cont, (1,)).astype(jnp.float32)
    return jnp.concatenate([first, (seg[1:] != seg[:-1]).astype(jnp.float32)])

def ssd_block(inner, bmat, cmat, step, decay, skip, seg, cont, carry_in):
    length, heads, head_size = inner.shape
    blocks = length // SPAN
    fresh = fresh_flags(seg, cont)

    def advance(carry, piece):
        part_x, part_b, part_c, part_dt, part_seg, part_fresh = piece
        logs = jnp.cumsum(part_dt * decay[None, :], axis=0)
        order = jnp.arange(SPAN)
        allowed = (order[:, None] >= order[None, :]) & (part_seg[:, None] == part_seg[None, :])
        gap = logs[:, None, :] - logs[None, :, :]
        weights = jnp.where(allowed[:, :, None], jnp.exp(jnp.where(allowed[:, :, None], gap, 0.0)), 0.0)
        scores = jnp.dot(part_c, part_b.T, precision=HIGH)
        scaled = part_x * part_dt[:, :, None]
        local = jnp.einsum('tsh,shp->thp', weights * scores[:, :, None], scaled, precision=HIGH)
        alive = (jnp.cumsum(part_fresh) == 0.0).astype(jnp.float32)
        into = alive[:, None] * jnp.exp(logs)
        carried = into[:, :, None] * jnp.einsum('tn,hpn->thp', part_c, carry, precision=HIGH)
        tail = jnp.exp(logs[-1][None, :] - logs) * (part_seg == part_seg[-1]).astype(jnp.float32)[:, None]
        update = jnp.einsum('shp,sn->hpn', scaled * tail[:, :, None], part_b, precision=HIGH)
        return (into[-1][:, None, None] * carry + update, local + carried)
    pieces = (inner.reshape(blocks, SPAN, heads, head_size), bmat.reshape(blocks, SPAN, -1), cmat.reshape(blocks, SPAN, -1), step.reshape(blocks, SPAN, heads), seg.reshape(blocks, SPAN), fresh.reshape(blocks, SPAN))
    final, outputs = lax.scan(advance, carry_in, pieces)
    return (outputs.reshape(length, heads, head_size) + skip[None, :, None] * inner, final)

def contract_rows(left, right):
    return lax.dot_general(left, right, (((0,), (0,)), ((), ())), preferred_element_type=jnp.float32)

def contract_cols(left, right):
    return lax.dot_general(left, right, (((1,), (1,)), ((), ())), preferred_element_type=jnp.float32)

def layer_forward(hidden, seg, params):
    prenorm, gate_w, inner_w, state_w, step_w, inner_kernel, inner_offset, state_kernel, state_offset, step_bias, decay_log, skip_gain, norm_gain, mixer_w = params
    length = hidden.shape[0]
    normed = rms_apply(hidden, prenorm).astype(jnp.bfloat16)
    gate = jnp.dot(normed, gate_w, preferred_element_type=jnp.float32)
    raw = jnp.concatenate([jnp.dot(normed, inner_w, preferred_element_type=jnp.float32).astype(jnp.bfloat16), jnp.dot(normed, state_w, preferred_element_type=jnp.float32).astype(jnp.bfloat16)], 1)
    step_raw = jnp.dot(normed, step_w, preferred_element_type=jnp.float32)
    taps = inner_kernel.shape[0]
    padded = jnp.concatenate([jnp.zeros((taps - 1, raw.shape[1]), jnp.bfloat16), raw], 0).astype(jnp.float32)
    seg_padded = jnp.concatenate([jnp.full((taps - 1,), -1, jnp.int32), seg.astype(jnp.int32)])
    kernel = jnp.concatenate([inner_kernel, state_kernel], 1)
    offset = jnp.concatenate([inner_offset, state_offset])
    act = conv_apply(padded, seg_padded, kernel, offset)
    inner = act[:, :INNER].reshape(length, HEADS, HEADDIM)
    bmat = act[:, INNER:INNER + STATE]
    cmat = act[:, INNER + STATE:]
    step = jax.nn.softplus(step_raw + step_bias)
    decay = -jnp.exp(decay_log)
    zeros_state = jnp.zeros((HEADS, HEADDIM, STATE), jnp.float32)
    mixed, _ = ssd_block(inner, bmat, cmat, step, decay, skip_gain, seg, 0.0, zeros_state)
    mixed = mixed.reshape(length, INNER)
    gated = mixed * jax.nn.silu(gate)
    scale = lax.rsqrt(lax.optimization_barrier(jnp.mean(gated * gated, axis=1)) + EPSILON)
    normout = (gated * scale[:, None] * norm_gain).astype(jnp.bfloat16)
    result = hidden + contract_cols(normout, mixer_w)
    return (result, (hidden, normed, gate, padded, seg_padded, step_raw, mixed, gated, scale, normout))

def layer_backward(back, seg, keep, params):
    prenorm, gate_w, inner_w, state_w, step_w, inner_kernel, inner_offset, state_kernel, state_offset, step_bias, decay_log, skip_gain, norm_gain, mixer_w = params
    hidden, normed, gate, padded, seg_padded, step_raw, mixed, gated, scale, normout = keep
    length = hidden.shape[0]
    back_b = back.astype(jnp.bfloat16)
    d_out = jnp.dot(back_b, mixer_w, preferred_element_type=jnp.float32)
    mixer_grad = contract_rows(back_b, normout)
    norm_grad = lax.optimization_barrier(jnp.sum(d_out * gated * scale[:, None], 0))
    inner_total = lax.optimization_barrier(jnp.sum(d_out * norm_gain * gated, 1))
    d_gated = scale[:, None] * norm_gain * d_out - gated * (scale ** 3 * inner_total / INNER)[:, None]
    sigma = jax.nn.sigmoid(gate)
    d_mixed = d_gated * gate * sigma
    d_gate = (d_gated * mixed * sigma * (1.0 + gate * (1.0 - sigma))).astype(jnp.bfloat16)
    kernel = jnp.concatenate([inner_kernel, state_kernel], 1)
    offset = jnp.concatenate([inner_offset, state_offset])
    act, conv_pull = jax.vjp(lambda pad, ker, off: conv_apply(pad, seg_padded, ker, off), padded, kernel, offset)
    inner = act[:, :INNER].reshape(length, HEADS, HEADDIM)
    bmat = act[:, INNER:INNER + STATE]
    cmat = act[:, INNER + STATE:]
    step = jax.nn.softplus(step_raw + step_bias)
    decay = -jnp.exp(decay_log)
    zeros_state = jnp.zeros((HEADS, HEADDIM, STATE), jnp.float32)

    def mixer_local(inner_v, bmat_v, cmat_v, step_v, decay_v, skip_v):
        return ssd_block(inner_v, bmat_v, cmat_v, step_v, decay_v, skip_v, seg, 0.0, zeros_state)[0]
    _, ssd_pull = jax.vjp(mixer_local, inner, bmat, cmat, step, decay, skip_gain)
    g_inner, g_bmat, g_cmat, g_step, g_decay, skip_grad = ssd_pull(d_mixed.reshape(length, HEADS, HEADDIM))
    g_act = jnp.concatenate([g_inner.reshape(length, INNER), g_bmat, g_cmat], 1)
    g_padded, kernel_grad, offset_grad = conv_pull(g_act)
    taps = inner_kernel.shape[0]
    g_raw = g_padded[taps - 1:]
    g_step_raw = g_step * jax.nn.sigmoid(step_raw + step_bias)
    g_inner_b = g_raw[:, :INNER].astype(jnp.bfloat16)
    g_state_b = g_raw[:, INNER:].astype(jnp.bfloat16)
    g_step_b = g_step_raw.astype(jnp.bfloat16)
    d_normed = contract_cols(d_gate, gate_w) + contract_cols(g_inner_b, inner_w) + contract_cols(g_step_b, step_w) + contract_cols(g_state_b, state_w)
    _, norm_pull = jax.vjp(rms_apply, hidden, prenorm)
    d_hidden, prenorm_grad = norm_pull(d_normed)
    grads = (prenorm_grad, contract_rows(normed, d_gate), contract_rows(normed, g_inner_b), contract_rows(normed, g_state_b), contract_rows(normed, g_step_b), kernel_grad[:, :INNER], offset_grad[:INNER], kernel_grad[:, INNER:], offset_grad[INNER:], lax.optimization_barrier(jnp.sum(g_step_raw, 0)), g_decay * decay, skip_grad, norm_grad, mixer_grad)
    return (back + d_hidden, grads)

def reference(tokens, segments, cotangent, prenorm, gate_proj, inner_proj, state_proj, step_proj, inner_kernel, inner_offset, state_kernel, state_offset, step_bias, decay_log, skip_gain, norm_gain, mixer_out):
    params_all = (prenorm, gate_proj, inner_proj, state_proj, step_proj, inner_kernel, inner_offset, state_kernel, state_offset, step_bias, decay_log, skip_gain, norm_gain, mixer_out)

    def layer_params(index):
        return tuple((param[index] for param in params_all))
    zero_totals = tuple((jnp.zeros(param.shape, jnp.float32) for param in params_all))

    def per_group(totals, piece):
        group_tokens, seg, group_cot = piece
        hidden = group_tokens.astype(jnp.float32)
        saved = []
        for index in range(LAYERS):
            hidden, keep = layer_forward(hidden, seg, layer_params(index))
            saved.append(keep)
        back = group_cot
        layer_grads = [None] * LAYERS
        for index in reversed(range(LAYERS)):
            back, layer_grads[index] = layer_backward(back, seg, saved[index], layer_params(index))
        stacked = tuple((jnp.stack([layer_grads[layer][member] for layer in range(LAYERS)]) for member in range(len(params_all))))
        totals = tuple((first + second for first, second in zip(totals, stacked)))
        return (totals, (hidden, back))
    totals, (outs, backs) = lax.scan(per_group, zero_totals, (tokens.reshape(GROUPS, GROUP_TOK, D), segments, cotangent.reshape(GROUPS, GROUP_TOK, D)))
    return (outs.reshape(TOKENS, D), backs.reshape(TOKENS, D), totals[0], totals[1], totals[2], totals[3], totals[4], totals[5], totals[6], totals[7], totals[8], totals[9], totals[10], totals[11], totals[12], totals[13])
```

```python
import functools

import jax
import jax.numpy as jnp
from jax import lax
from jax.experimental import pallas as pl
from jax.experimental.pallas import tpu as pltpu
from jax.sharding import PartitionSpec as P

SPAN = 128


EPSILON = 1e-05
HIGH = lax.Precision.HIGHEST


def passed_along(block, axis, distance):
    devices = range(lax.axis_size(axis))
    route = [(i - distance, i) for i in devices if i - distance in devices]
    return lax.ppermute(block, axis, route)


def prefix(shard, axis, join, neutral):
    place = lax.axis_index(axis)
    gathered = jax.tree.map(
        lambda a, kind: lax.all_gather(a.astype(kind), axis), shard, (jnp.bfloat16, jnp.bfloat16)
    )
    state = jax.tree.map(lambda a, e: jnp.zeros_like(a) + jnp.asarray(e, a.dtype), shard, neutral)

    def prefix_one(turn, state):
        return join(
            state,
            jax.tree.map(
                lambda a, own: lax.dynamic_index_in_dim(a, turn, 0, False).astype(own.dtype),
                gathered,
                shard,
            ),
        )

    return lax.fori_loop(0, place, prefix_one, state)


def entering(shard, axis, join, neutral):
    count = lax.axis_size(axis)
    place = lax.axis_index(axis)
    ahead = count - 1 - place
    gathered = jax.tree.map(
        lambda a, kind: lax.all_gather(a.astype(kind), axis),
        shard,
        jax.tree.map(lambda a: jnp.bfloat16 if a.dtype == jnp.float32 else a.dtype, shard),
    )
    state = jax.tree.map(lambda a, e: jnp.zeros_like(a) + jnp.asarray(e, a.dtype), shard, neutral)

    def entering_one(turn, state):
        source = count - 1 - turn
        return join(
            state,
            jax.tree.map(
                lambda a, own: lax.dynamic_index_in_dim(a, source, 0, False).astype(own.dtype),
                gathered,
                shard,
            ),
        )

    return lax.fori_loop(0, ahead, entering_one, state)


def rms_apply(hidden, gain):
    inverse = lax.rsqrt(jnp.mean(hidden * hidden, axis=-1, keepdims=True) + EPSILON)
    return hidden * inverse * gain


def conv_apply(padded, seg_padded, kernel, offset):
    taps = kernel.shape[0]
    length = padded.shape[0] - taps + 1
    current = seg_padded[taps - 1 :]
    total = jnp.zeros((length, padded.shape[1]), jnp.float32) + offset
    for shift_index in range(taps):
        same = (seg_padded[shift_index : shift_index + length] == current).astype(jnp.float32)
        total = (
            total + kernel[shift_index] * padded[shift_index : shift_index + length] * same[:, None]
        )
    return jax.nn.silu(total)


def fresh_flags(seg, cont):
    first = jnp.reshape(1.0 - cont, (1,))
    return jnp.concatenate([first, (seg[1:] != seg[:-1]).astype(jnp.float32)])


def inflow(step, decay, seg, cont):
    alive = (jnp.cumsum(fresh_flags(seg, cont)) == 0.0).astype(jnp.float32)
    return alive[:, None] * jnp.exp(jnp.cumsum(step * decay[None, :], axis=0))


def ssd_block(inner, bmat, cmat, step, decay, skip, seg, cont, carry_in):
    length, heads, head_size = inner.shape
    blocks = length // SPAN
    fresh = fresh_flags(seg, cont)

    def advance(carry, piece):
        part_x, part_b, part_c, part_dt, part_seg, part_fresh = piece
        logs = jnp.cumsum(part_dt * decay[None, :], axis=0)
        order = jnp.arange(SPAN)
        allowed = (order[:, None] >= order[None, :]) & (part_seg[:, None] == part_seg[None, :])
        gap = logs[:, None, :] - logs[None, :, :]
        weights = jnp.where(
            allowed[:, :, None], jnp.exp(jnp.where(allowed[:, :, None], gap, 0.0)), 0.0
        )
        scores = jnp.dot(part_c, part_b.T, precision=HIGH)
        scaled = part_x * part_dt[:, :, None]
        local = jnp.einsum("tsh,shp->thp", weights * scores[:, :, None], scaled, precision=HIGH)
        alive = (jnp.cumsum(part_fresh) == 0.0).astype(jnp.float32)
        into = alive[:, None] * jnp.exp(logs)
        carried = into[:, :, None] * jnp.einsum("tn,hpn->thp", part_c, carry, precision=HIGH)
        tail = (
            jnp.exp(logs[-1][None, :] - logs)
            * (part_seg == part_seg[-1]).astype(jnp.float32)[:, None]
        )
        update = jnp.einsum("shp,sn->hpn", scaled * tail[:, :, None], part_b, precision=HIGH)
        return (into[-1][:, None, None] * carry + update, local + carried)

    pieces = (
        inner.reshape(blocks, SPAN, heads, head_size),
        bmat.reshape(blocks, SPAN, -1),
        cmat.reshape(blocks, SPAN, -1),
        step.reshape(blocks, SPAN, heads),
        seg.reshape(blocks, SPAN),
        fresh.reshape(blocks, SPAN),
    )
    final, outputs = lax.scan(advance, carry_in, pieces)
    return (outputs.reshape(length, heads, head_size) + skip[None, :, None] * inner, final)


def link(earlier, later):
    return (earlier[0] * later[0], later[0][:, None, None] * earlier[1] + later[1])


def contract_cols(left, right):
    return lax.dot_general(
        left, right, (((1,), (1,)), ((), ())), preferred_element_type=jnp.float32
    )


def project(normed, weight, feat_dim):
    return lax.dot_general(
        normed, weight, (((feat_dim,), (0,)), ((), ())), preferred_element_type=jnp.float32
    )


def grad_rows(normed, delta, feat_dim):
    return lax.dot_general(
        normed, delta, (((1 - feat_dim,), (0,)), ((), ())), preferred_element_type=jnp.float32
    )


MESH = pl.DeviceIdType.MESH
VM = pl.BlockSpec(memory_space=pltpu.VMEM)


def remote(src, dst, send, recv, where):
    return pltpu.make_async_remote_copy(
        src_ref=src, dst_ref=dst, send_sem=send, recv_sem=recv, device_id=where, device_id_type=MESH
    )


def greet(peers):
    barrier = pltpu.get_barrier_semaphore()
    for peer in peers:
        pl.semaphore_signal(barrier, inc=1, device_id=peer, device_id_type=MESH)
    pl.semaphore_wait(barrier, len(peers))


def weights_kernel(nz, ny, *refs):
    shards, (win, wmix), (own_sem, zsend, zrecv, ysend, yrecv) = refs[:4], refs[4:6], refs[6:]
    z, y = lax.axis_index("fsdp"), lax.axis_index("ctx")
    rows, cols = shards[0].shape[1:]
    z_at = lambda d: lax.rem(z + d, nz)
    y_at = lambda e: lax.rem(y + e, ny)
    greet([{"fsdp": z_at(d)} for d in range(1, nz)] + [{"ctx": y_at(e)} for e in range(1, ny)])

    def region(piece, zs, ys):
        at = pl.ds(pl.multiple_of((zs * ny + ys) * rows, rows), rows)
        if piece == 3:
            return wmix.at[:, at, :]
        return win.at[:, at, pl.ds(piece * cols, cols)]

    own, sends = [], []
    for piece in range(4):
        copy = pltpu.make_async_copy(shards[piece], region(piece, z, y), own_sem.at[piece])
        copy.start()
        own.append(copy)
    zcopies, ycopies = {}, {}
    for piece in range(4):
        for d in range(1, nz):
            copy = remote(
                shards[piece],
                region(piece, z, y),
                zsend.at[piece, d - 1],
                zrecv.at[piece, d - 1],
                {"fsdp": z_at(d)},
            )
            copy.start()
            zcopies[piece, d] = copy
        for e in range(1, ny):
            copy = remote(
                shards[piece],
                region(piece, z, y),
                ysend.at[piece, 0, e - 1],
                yrecv.at[piece, 0, e - 1],
                {"ctx": y_at(e)},
            )
            copy.start()
            ycopies[piece, 0, e] = copy
    for piece in range(4):
        for d in range(1, nz):
            zcopies[piece, d].wait_recv()
            block = region(piece, z_at(nz - d), y)
            for e in range(1, ny):
                copy = remote(
                    block,
                    block,
                    ysend.at[piece, d, e - 1],
                    yrecv.at[piece, d, e - 1],
                    {"ctx": y_at(e)},
                )
                copy.start()
                ycopies[piece, d, e] = copy
    for copy in own:
        copy.wait()
    for copy in zcopies.values():
        copy.wait_send()
    for copy in ycopies.values():
        copy.wait()


def gather_weights(gate, inner, extra, mixer):
    nz, ny = lax.axis_size("fsdp"), lax.axis_size("ctx")
    layers, rows, cols = gate.shape
    full = rows * nz * ny
    dma = pltpu.SemaphoreType.DMA
    return pl.pallas_call(
        functools.partial(weights_kernel, nz, ny),
        out_shape=(
            jax.ShapeDtypeStruct((layers, full, 3 * cols), gate.dtype),
            jax.ShapeDtypeStruct((layers, full, cols), gate.dtype),
        ),
        in_specs=[VM] * 4,
        out_specs=(VM, VM),
        scratch_shapes=[
            dma((4,)),
            dma((4, nz - 1)),
            dma((4, nz - 1)),
            dma((4, nz, ny - 1)),
            dma((4, nz, ny - 1)),
        ],
        compiler_params=pltpu.CompilerParams(collective_id=1, has_side_effects=True),
        name="weights",
    )(gate, inner, extra, mixer)


def grads_kernel(nz, layers, *refs):
    ins = refs[: 2 * layers]
    small = refs[2 * layers]
    outs = refs[2 * layers + 1 : 2 * layers + 5]
    small_out = refs[2 * layers + 5]
    rest = refs[2 * layers + 6 :]
    yin, ymix, pin, pmix, zin, zmix, srecv = rest[:7]
    ysend, yrecv, zsend, zrecv, ssend, srec, sown = rest[7:]
    ny = 2
    z, y = lax.axis_index("fsdp"), lax.axis_index("ctx")
    other = 1 - y
    rows, cols = outs[0].shape[1:]
    z_at = lambda d: lax.rem(z + d, nz)
    peers = []
    for d in range(nz):
        for where in (y, other):
            if not (d == 0 and where is y):
                peers.append({"fsdp": z_at(d), "ctx": where})
    greet(peers)
    me = z * ny + y
    keep = pltpu.make_async_copy(small, srecv.at[me], sown)
    keep.start()

    def chunk(zd, yd):
        return pl.ds(pl.multiple_of((zd * ny + yd) * rows, rows), rows)

    order = [(layer, d) for layer in range(layers) for d in list(range(1, nz)) + [0]]
    ycopies, zcopies, scopies = {}, {}, []
    for layer, d in order:
        at = chunk(z_at(d), other)
        for which, buffer in enumerate((yin, ymix)):
            copy = remote(
                ins[2 * layer + which].at[at, :],
                buffer.at[layer, d],
                ysend.at[layer, d, which],
                yrecv.at[layer, d, which],
                {"ctx": other},
            )
            copy.start()
            ycopies[layer, d, which] = copy
    for i, peer in enumerate(peers):
        copy = remote(small, srecv.at[me], ssend.at[i], srec.at[i], peer)
        copy.start()
        scopies.append(copy)
    for layer, d in order:
        at = chunk(z_at(d), y)
        for which, (got, put, land) in enumerate(((yin, pin, zin), (ymix, pmix, zmix))):
            ycopies[layer, d, which].wait_recv()
            total = ins[2 * layer + which][at, :].astype(jnp.float32) + got[layer, d].astype(
                jnp.float32
            )
            if d:
                put[layer, d - 1] = total.astype(jnp.bfloat16)
                copy = remote(
                    put.at[layer, d - 1],
                    land.at[layer, d - 1],
                    zsend.at[layer, d - 1, which],
                    zrecv.at[layer, d - 1, which],
                    {"fsdp": z_at(d)},
                )
                copy.start()
                zcopies[layer, d, which] = copy
            elif which:
                outs[3][layer] = total
            else:
                for part in range(3):
                    outs[part][layer] = total[:, part * cols : (part + 1) * cols]
    for layer in range(layers):
        for d in range(1, nz):
            zcopies[layer, d, 0].wait_recv()
            zcopies[layer, d, 1].wait_recv()
        for part in range(3):
            total = outs[part][layer]
            for d in range(1, nz):
                total = total + zin[layer, d - 1, :, part * cols : (part + 1) * cols].astype(
                    jnp.float32
                )
            outs[part][layer] = total
        total = outs[3][layer]
        for d in range(1, nz):
            total = total + zmix[layer, d - 1].astype(jnp.float32)
        outs[3][layer] = total
    keep.wait()
    for copy in scopies:
        copy.wait_recv()
    total = srecv[0]
    for i in range(1, nz * ny):
        total = total + srecv[i]
    small_out[...] = total
    for copy in list(ycopies.values()) + list(zcopies.values()) + scopies:
        copy.wait_send()


def reduce_grads(grads, small):
    nz = lax.axis_size("fsdp")
    layers = len(grads) // 2
    full, cols = grads[1].shape
    rows = full // (2 * nz)
    dma, bf = pltpu.SemaphoreType.DMA, jnp.bfloat16
    return pl.pallas_call(
        functools.partial(grads_kernel, nz, layers),
        out_shape=tuple(jax.ShapeDtypeStruct((layers, rows, cols), jnp.float32) for _ in range(4))
        + (jax.ShapeDtypeStruct(small.shape, jnp.float32),),
        in_specs=[VM] * (2 * layers + 1),
        out_specs=(VM,) * 5,
        scratch_shapes=[
            pltpu.VMEM((layers, nz, rows, 3 * cols), bf),
            pltpu.VMEM((layers, nz, rows, cols), bf),
            pltpu.VMEM((layers, nz - 1, rows, 3 * cols), bf),
            pltpu.VMEM((layers, nz - 1, rows, cols), bf),
            pltpu.VMEM((layers, nz - 1, rows, 3 * cols), bf),
            pltpu.VMEM((layers, nz - 1, rows, cols), bf),
            pltpu.VMEM((2 * nz,) + small.shape, jnp.float32),
            dma((layers, nz, 2)),
            dma((layers, nz, 2)),
            dma((layers, nz - 1, 2)),
            dma((layers, nz - 1, 2)),
            dma((2 * nz - 1,)),
            dma((2 * nz - 1,)),
            dma,
        ],
        compiler_params=pltpu.CompilerParams(collective_id=2, has_side_effects=True),
        name="grads",
    )(*grads, small)


def sum_kernel(n, tallied, *refs):
    if tallied:
        x, tally, out, tally_out, got, put, seen = refs[:7]
        send, recv, send2, recv2, tsend, trecv, town = refs[7:]
    else:
        x, out, got, put, send, recv, send2, recv2 = refs
    me = lax.axis_index("tp")
    rows = x.shape[0] // n
    at = lambda i: pl.ds(pl.multiple_of(i * rows, rows), rows)
    peers = [lax.rem(me + d, n) for d in range(1, n)]
    greet([{"tp": peer} for peer in peers])
    first, second, tallies = [], [], []
    for d, peer in enumerate(peers):
        copy = remote(x.at[at(peer), :], got.at[d], send.at[d], recv.at[d], {"tp": peer})
        copy.start()
        first.append(copy)
    if tallied:
        keep = pltpu.make_async_copy(tally, seen.at[me], town)
        keep.start()
        for d, peer in enumerate(peers):
            copy = remote(tally, seen.at[me], tsend.at[d], trecv.at[d], {"tp": peer})
            copy.start()
            tallies.append(copy)
    total = x[at(me), :].astype(jnp.float32)
    for d in range(n - 1):
        first[d].wait_recv()
        total = total + got[d].astype(jnp.float32)
    put[...] = total.astype(put.dtype)
    for d, peer in enumerate(peers):
        copy = remote(put, out.at[at(me), :], send2.at[d], recv2.at[d], {"tp": peer})
        copy.start()
        second.append(copy)
    out[at(me), :] = total.astype(put.dtype)
    if tallied:
        keep.wait()
        for copy in tallies:
            copy.wait_recv()
        total = seen[0]
        for i in range(1, n):
            total = total + seen[i]
        tally_out[...] = total
    for copy in second:
        copy.wait_recv()
    for copy in first + second + tallies:
        copy.wait_send()


def tp_sum(x, ident, tally=None):
    n = lax.axis_size("tp")
    rows, cols = x.shape
    dma = pltpu.SemaphoreType.DMA
    tallied = tally is not None
    block = pltpu.VMEM((n - 1, rows // n, cols), x.dtype)
    scratch = [block, pltpu.VMEM((rows // n, cols), x.dtype)]
    shape = jax.ShapeDtypeStruct(x.shape, x.dtype)
    if tallied:
        scratch.append(pltpu.VMEM((n,) + tally.shape, jnp.float32))
        shape = (shape, jax.ShapeDtypeStruct(tally.shape, jnp.float32))
    scratch += [dma((n - 1,))] * (6 if tallied else 4) + ([dma] if tallied else [])
    return pl.pallas_call(
        functools.partial(sum_kernel, n, tallied),
        out_shape=shape,
        in_specs=[VM] * (2 if tallied else 1),
        out_specs=(VM, VM) if tallied else VM,
        scratch_shapes=scratch,
        compiler_params=pltpu.CompilerParams(collective_id=ident, has_side_effects=True),
        name="tpsum",
    )(*((x, tally) if tallied else (x,)))


def body(
    tokens,
    segments,
    cotangent,
    prenorm,
    gate_proj,
    inner_proj,
    state_proj,
    step_proj,
    inner_kernel,
    inner_offset,
    state_kernel,
    state_offset,
    step_bias,
    decay_log,
    skip_gain,
    norm_gain,
    mixer_out,
):
    length = tokens.shape[0]
    model = tokens.shape[1]
    layers = gate_proj.shape[0]
    taps = inner_kernel.shape[1]
    inner_local = gate_proj.shape[2]
    heads_local = step_proj.shape[2]
    head_size = inner_local // heads_local
    state_size = state_proj.shape[2] // 2
    inner_all = inner_local * lax.axis_size("tp")
    feat = model // lax.axis_size("tp")
    feat_start = lax.axis_index("tp") * feat
    start = lax.axis_index("ctx") * length
    seg_pad = jnp.concatenate([jnp.full((taps - 1,), -1, jnp.int32), segments[0]])
    seg_padded = lax.dynamic_slice_in_dim(seg_pad, start, length + taps - 1)
    seg_here = seg_padded[taps - 1 :]
    cont = (seg_padded[taps - 2] == seg_padded[taps - 1]).astype(jnp.float32)
    zeros_state = jnp.zeros((heads_local, head_size, state_size), jnp.float32)
    identity = (jnp.ones((heads_local,), jnp.float32), zeros_state)

    def layer_kernel(layer):
        kernel = jnp.concatenate([inner_kernel[layer], state_kernel[layer]], 1)
        offset = jnp.concatenate([inner_offset[layer], state_offset[layer]])
        return (kernel, offset)

    def split_act(act, layer):
        inner = act[:, :inner_local].reshape(length, heads_local, head_size)
        bmat = act[:, inner_local : inner_local + state_size]
        cmat = act[:, inner_local + state_size :]
        step = jax.nn.softplus(kept_step[layer] + step_bias[layer])
        return (inner, bmat, cmat, step)

    feat_dim = 1
    hidden = tokens.astype(jnp.float32)
    back = cotangent
    kept = []
    kept_step = []
    for layer in range(layers):
        mats = (
            lax.all_gather(gate_proj[layer], ("fsdp", "ctx"), axis=0, tiled=True),
            lax.all_gather(inner_proj[layer], ("fsdp", "ctx"), axis=0, tiled=True),
            lax.all_gather(state_proj[layer], ("fsdp", "ctx"), axis=0, tiled=True),
            lax.all_gather(step_proj[layer], ("fsdp", "ctx"), axis=0, tiled=True),
            lax.all_gather(mixer_out[layer], ("fsdp", "ctx"), axis=0, tiled=True),
        )
        gate_w, inner_w, state_w, step_w, mixer_w = mats
        inverse = None
        normed = rms_apply(hidden, prenorm[layer]).astype(jnp.bfloat16)
        gate = project(normed, gate_w, feat_dim)
        raw = jnp.concatenate(
            [
                project(normed, inner_w, feat_dim).astype(jnp.bfloat16),
                project(normed, state_w, feat_dim).astype(jnp.bfloat16),
            ],
            1,
        )
        step_raw = project(normed, step_w, feat_dim)
        kept_step.append(step_raw)
        before = passed_along(raw[length - (taps - 1) :], "ctx", 1)
        padded = jnp.concatenate([before, raw], 0).astype(jnp.float32)
        kernel, offset = layer_kernel(layer)
        act = conv_apply(padded, seg_padded, kernel, offset)
        inner, bmat, cmat, step = split_act(act, layer)
        decay = -jnp.exp(decay_log[layer])
        partial_mixed, produced = ssd_block(
            inner, bmat, cmat, step, decay, skip_gain[layer], seg_here, cont, zeros_state
        )
        flow = inflow(step, decay, seg_here, cont)
        incoming = prefix((flow[-1], produced), "ctx", link, identity)[1]
        mixed = partial_mixed + jnp.einsum("th,tn,hpn->thp", flow, cmat, incoming, precision=HIGH)
        mixed = mixed.reshape(length, inner_local)
        gated = mixed * jax.nn.silu(gate)
        squares = lax.psum(jnp.sum(gated * gated, 1), "tp")
        scale = lax.rsqrt(squares / inner_all + EPSILON)
        normout = (gated * scale[:, None] * norm_gain[layer]).astype(jnp.bfloat16)
        projected = lax.psum(contract_cols(normout, mixer_w), "tp")
        stored = None
        kept.append(
            (hidden, inverse, stored, normed, gate, padded, incoming, mixed, gated, scale, normout)
        )
        hidden = hidden + projected
    output = hidden
    shard_grads = [None] * layers
    small_grads = [None] * layers
    for layer in reversed(range(layers)):
        hidden_in, inverse, stored, normed, gate, padded, incoming, mixed, gated, scale, normout = (
            kept[layer]
        )
        mats = (
            lax.all_gather(gate_proj[layer], ("fsdp", "ctx"), axis=0, tiled=True),
            lax.all_gather(inner_proj[layer], ("fsdp", "ctx"), axis=0, tiled=True),
            lax.all_gather(state_proj[layer], ("fsdp", "ctx"), axis=0, tiled=True),
            lax.all_gather(step_proj[layer], ("fsdp", "ctx"), axis=0, tiled=True),
            lax.all_gather(mixer_out[layer], ("fsdp", "ctx"), axis=0, tiled=True),
        )
        gate_w, inner_w, state_w, step_w, mixer_w = mats
        gain = norm_gain[layer]
        back_b = back.astype(jnp.bfloat16)
        d_out = project(back_b, mixer_w, feat_dim)
        mixer_grad = grad_rows(back_b, normout, feat_dim)
        norm_grad = jnp.sum(d_out * gated * scale[:, None], 0)
        inner_total = lax.psum(jnp.sum(d_out * gain * gated, 1), "tp")
        d_gated = (
            scale[:, None] * gain * d_out - gated * (scale**3 * inner_total / inner_all)[:, None]
        )
        sigma = jax.nn.sigmoid(gate)
        d_mixed = d_gated * gate * sigma
        d_gate = (d_gated * mixed * sigma * (1.0 + gate * (1.0 - sigma))).astype(jnp.bfloat16)
        kernel, offset = layer_kernel(layer)
        act, conv_pull = jax.vjp(
            lambda pad, ker, off: conv_apply(pad, seg_padded, ker, off), padded, kernel, offset
        )
        inner, bmat, cmat, step = split_act(act, layer)
        decay = -jnp.exp(decay_log[layer])
        flow = inflow(step, decay, seg_here, cont)
        d_mixed3 = d_mixed.reshape(length, heads_local, head_size)
        adjoint = jnp.einsum("th,thp,tn->hpn", flow, d_mixed3, cmat, precision=HIGH)
        carried = entering((flow[-1], adjoint), "ctx", link, identity)[1]

        def mixer_local(inner_v, bmat_v, cmat_v, step_v, decay_v, skip_v, entry):
            part_v, produced_v = ssd_block(
                inner_v, bmat_v, cmat_v, step_v, decay_v, skip_v, seg_here, cont, zeros_state
            )
            flow_v = inflow(step_v, decay_v, seg_here, cont)
            result_v = part_v + jnp.einsum("th,tn,hpn->thp", flow_v, cmat_v, entry, precision=HIGH)
            return (result_v, flow_v[-1][:, None, None] * entry + produced_v)

        _, ssd_pull = jax.vjp(
            mixer_local, inner, bmat, cmat, step, decay, skip_gain[layer], incoming
        )
        g_inner, g_bmat, g_cmat, g_step, g_decay, skip_grad, _ = ssd_pull((d_mixed3, carried))
        g_state = lax.psum(jnp.concatenate([g_bmat, g_cmat], 1).astype(jnp.bfloat16), "tp").astype(
            jnp.float32
        )
        g_act = jnp.concatenate([g_inner.reshape(length, inner_local), g_state], 1)
        g_padded, kernel_grad, offset_grad = conv_pull(g_act)
        returned = passed_along(g_padded[: taps - 1], "ctx", -1)
        g_raw = g_padded[taps - 1 :] + jnp.concatenate(
            [jnp.zeros((length - (taps - 1), g_padded.shape[1]), jnp.float32), returned], 0
        )
        g_step_raw = g_step * jax.nn.sigmoid(kept_step[layer] + step_bias[layer])
        g_inner_b = g_raw[:, :inner_local].astype(jnp.bfloat16)
        g_state_b = g_raw[:, inner_local:].astype(jnp.bfloat16)
        g_step_b = g_step_raw.astype(jnp.bfloat16)
        partial_normed = (
            contract_cols(d_gate, gate_w)
            + contract_cols(g_inner_b, inner_w)
            + contract_cols(g_step_b, step_w)
        )
        d_normed = lax.psum(partial_normed.astype(jnp.bfloat16), "tp").astype(
            jnp.float32
        ) + contract_cols(g_state_b, state_w)
        _, norm_pull = jax.vjp(rms_apply, hidden_in, prenorm[layer])
        d_hidden, prenorm_full = norm_pull(d_normed)
        prenorm_grad = lax.dynamic_slice_in_dim(prenorm_full, feat_start, feat)
        shard_grads[layer] = (
            lax.psum_scatter(
                grad_rows(normed, d_gate, feat_dim),
                ("fsdp", "ctx"),
                scatter_dimension=0,
                tiled=True,
            ),
            lax.psum_scatter(
                grad_rows(normed, g_inner_b, feat_dim),
                ("fsdp", "ctx"),
                scatter_dimension=0,
                tiled=True,
            ),
            lax.psum_scatter(
                grad_rows(normed, g_state_b, feat_dim),
                ("fsdp", "ctx"),
                scatter_dimension=0,
                tiled=True,
            ),
            lax.psum_scatter(
                grad_rows(normed, g_step_b, feat_dim),
                ("fsdp", "ctx"),
                scatter_dimension=0,
                tiled=True,
            ),
            lax.psum_scatter(mixer_grad, ("fsdp", "ctx"), scatter_dimension=0, tiled=True),
        )
        back = back + d_hidden
        small_grads[layer] = (
            prenorm_grad,
            kernel_grad[:, :inner_local],
            offset_grad[:inner_local],
            kernel_grad[:, inner_local:],
            offset_grad[inner_local:],
            jnp.sum(g_step_raw, 0),
            g_decay * decay,
            skip_grad,
            norm_grad,
        )
    output = lax.dynamic_slice_in_dim(output, feat_start, feat, 1)
    back = lax.dynamic_slice_in_dim(back, feat_start, feat, 1)

    def stack_member(groups, member):
        return jnp.stack([groups[layer][member] for layer in range(layers)])

    summed = lax.psum(
        (
            stack_member(small_grads, 0),
            stack_member(small_grads, 1),
            stack_member(small_grads, 2),
            stack_member(small_grads, 3),
            stack_member(small_grads, 4),
            stack_member(small_grads, 5),
            stack_member(small_grads, 6),
            stack_member(small_grads, 7),
            stack_member(small_grads, 8),
        ),
        ("fsdp", "ctx"),
    )
    return (
        output,
        back,
        summed[0],
        stack_member(shard_grads, 0),
        stack_member(shard_grads, 1),
        stack_member(shard_grads, 2),
        stack_member(shard_grads, 3),
        summed[1],
        summed[2],
        summed[3],
        summed[4],
        summed[5],
        summed[6],
        summed[7],
        summed[8],
        stack_member(shard_grads, 4),
    )


def body_kernels(
    tokens,
    segments,
    cotangent,
    prenorm,
    gate_proj,
    inner_proj,
    state_proj,
    step_proj,
    inner_kernel,
    inner_offset,
    state_kernel,
    state_offset,
    step_bias,
    decay_log,
    skip_gain,
    norm_gain,
    mixer_out,
):
    length = tokens.shape[0]
    model = tokens.shape[1]
    layers = gate_proj.shape[0]
    taps = inner_kernel.shape[1]
    inner_local = gate_proj.shape[2]
    heads_local = step_proj.shape[2]
    head_size = inner_local // heads_local
    state_size = state_proj.shape[2] // 2
    inner_all = inner_local * lax.axis_size("tp")
    feat = model // lax.axis_size("tp")
    feat_start = lax.axis_index("tp") * feat
    start = lax.axis_index("ctx") * length
    seg_pad = jnp.concatenate([jnp.full((taps - 1,), -1, jnp.int32), segments[0]])
    seg_padded = lax.dynamic_slice_in_dim(seg_pad, start, length + taps - 1)
    seg_here = seg_padded[taps - 1 :]
    cont = (seg_padded[taps - 2] == seg_padded[taps - 1]).astype(jnp.float32)
    zeros_state = jnp.zeros((heads_local, head_size, state_size), jnp.float32)
    identity = (jnp.ones((heads_local,), jnp.float32), zeros_state)

    def layer_kernel(layer):
        kernel = jnp.concatenate([inner_kernel[layer], state_kernel[layer]], 1)
        offset = jnp.concatenate([inner_offset[layer], state_offset[layer]])
        return (kernel, offset)

    def split_act(act, layer):
        inner = act[:, :inner_local].reshape(length, heads_local, head_size)
        bmat = act[:, inner_local : inner_local + state_size]
        cmat = act[:, inner_local + state_size :]
        step = jax.nn.softplus(kept_step[layer] + step_bias[layer])
        return (inner, bmat, cmat, step)

    feat_dim = 1
    hidden = tokens.astype(jnp.float32)
    back = cotangent
    kept = []
    kept_step = []
    cols = inner_local
    pad = cols - 2 * state_size - heads_local
    extra = jnp.concatenate(
        [state_proj, step_proj, jnp.zeros(step_proj.shape[:2] + (pad,), step_proj.dtype)], 2
    )
    win, wmix = gather_weights(gate_proj, inner_proj, extra, mixer_out)
    bf = jnp.bfloat16
    lead = (lax.axis_index("tp") == 0).astype(bf)
    for layer in range(layers):
        inverse = None
        normed = rms_apply(hidden, prenorm[layer]).astype(jnp.bfloat16)
        wide = project(normed, win[layer], feat_dim)
        gate = wide[:, :cols]
        raw = wide[:, cols : 2 * cols + 2 * state_size].astype(bf)
        step_raw = wide[:, 2 * cols + 2 * state_size :][:, :heads_local]
        kept_step.append(step_raw)
        before = passed_along(raw[length - (taps - 1) :], "ctx", 1)
        padded = jnp.concatenate([before, raw], 0).astype(jnp.float32)
        kernel, offset = layer_kernel(layer)
        act = conv_apply(padded, seg_padded, kernel, offset)
        inner, bmat, cmat, step = split_act(act, layer)
        decay = -jnp.exp(decay_log[layer])
        partial_mixed, produced = ssd_block(
            inner, bmat, cmat, step, decay, skip_gain[layer], seg_here, cont, zeros_state
        )
        flow = inflow(step, decay, seg_here, cont)
        incoming = passed_along(produced.astype(bf), "ctx", 1).astype(jnp.float32)
        mixed = partial_mixed + jnp.einsum("th,tn,hpn->thp", flow, cmat, incoming, precision=HIGH)
        mixed = mixed.reshape(length, inner_local)
        gated = mixed * jax.nn.silu(gate)
        squares = jnp.broadcast_to(jnp.sum(gated * gated, 1)[None], (8, length))
        lifted = (gated * norm_gain[layer]).astype(bf)
        projected, squares = tp_sum(contract_cols(lifted, wmix[layer]).astype(bf), 3, squares)
        projected = projected.astype(jnp.float32)
        scale = lax.rsqrt(squares[0] / inner_all + EPSILON)
        normout = (gated * scale[:, None] * norm_gain[layer]).astype(bf)
        stored = projected
        kept.append(
            (hidden, inverse, stored, normed, gate, padded, incoming, mixed, gated, scale, normout)
        )
        hidden = hidden + projected * scale[:, None]
    output = hidden
    shard_grads = [None] * layers
    small_grads = [None] * layers
    for layer in reversed(range(layers)):
        hidden_in, inverse, stored, normed, gate, padded, incoming, mixed, gated, scale, normout = (
            kept[layer]
        )
        gain = norm_gain[layer]
        back_b = back.astype(jnp.bfloat16)
        d_out = project(back_b, wmix[layer], feat_dim)
        mixer_grad = grad_rows(back_b, normout, feat_dim)
        norm_grad = jnp.sum(d_out * gated * scale[:, None], 0)
        inner_total = jnp.sum(back_b.astype(jnp.float32) * stored, 1)
        d_gated = (
            scale[:, None] * gain * d_out - gated * (scale**3 * inner_total / inner_all)[:, None]
        )
        sigma = jax.nn.sigmoid(gate)
        d_mixed = d_gated * gate * sigma
        d_gate = (d_gated * mixed * sigma * (1.0 + gate * (1.0 - sigma))).astype(jnp.bfloat16)
        kernel, offset = layer_kernel(layer)
        act, conv_pull = jax.vjp(
            lambda pad, ker, off: conv_apply(pad, seg_padded, ker, off), padded, kernel, offset
        )
        inner, bmat, cmat, step = split_act(act, layer)
        decay = -jnp.exp(decay_log[layer])
        flow = inflow(step, decay, seg_here, cont)
        d_mixed3 = d_mixed.reshape(length, heads_local, head_size)
        adjoint = jnp.einsum("th,thp,tn->hpn", flow, d_mixed3, cmat, precision=HIGH)
        carried = passed_along(adjoint.astype(bf), "ctx", -1).astype(jnp.float32)

        def mixer_local(inner_v, bmat_v, cmat_v, step_v, decay_v, skip_v, entry):
            part_v, produced_v = ssd_block(
                inner_v, bmat_v, cmat_v, step_v, decay_v, skip_v, seg_here, cont, zeros_state
            )
            flow_v = inflow(step_v, decay_v, seg_here, cont)
            result_v = part_v + jnp.einsum("th,tn,hpn->thp", flow_v, cmat_v, entry, precision=HIGH)
            return (result_v, flow_v[-1][:, None, None] * entry + produced_v)

        _, ssd_pull = jax.vjp(
            mixer_local, inner, bmat, cmat, step, decay, skip_gain[layer], incoming
        )
        g_inner, g_bmat, g_cmat, g_step, g_decay, skip_grad, _ = ssd_pull((d_mixed3, carried))
        g_state = tp_sum(jnp.concatenate([g_bmat, g_cmat], 1).astype(bf), 4).astype(jnp.float32)
        g_act = jnp.concatenate([g_inner.reshape(length, inner_local), g_state], 1)
        g_padded, kernel_grad, offset_grad = conv_pull(g_act)
        returned = passed_along(g_padded[: taps - 1], "ctx", -1)
        g_raw = g_padded[taps - 1 :] + jnp.concatenate(
            [jnp.zeros((length - (taps - 1), g_padded.shape[1]), jnp.float32), returned], 0
        )
        g_step_raw = g_step * jax.nn.sigmoid(kept_step[layer] + step_bias[layer])
        g_inner_b = g_raw[:, :inner_local].astype(jnp.bfloat16)
        g_state_b = g_raw[:, inner_local:].astype(jnp.bfloat16)
        g_step_b = g_step_raw.astype(jnp.bfloat16)
        blank = jnp.zeros((length, pad), bf)
        delta = jnp.concatenate([d_gate, g_inner_b, g_state_b, g_step_b, blank], 1)
        single = jnp.concatenate([d_gate, g_inner_b, g_state_b * lead, g_step_b, blank], 1)
        d_normed = tp_sum(contract_cols(single, win[layer]).astype(bf), 5).astype(jnp.float32)
        _, norm_pull = jax.vjp(rms_apply, hidden_in, prenorm[layer])
        d_hidden, prenorm_full = norm_pull(d_normed)
        prenorm_grad = lax.dynamic_slice_in_dim(prenorm_full, feat_start, feat)
        shard_grads[layer] = (
            grad_rows(normed, delta, feat_dim).astype(bf),
            mixer_grad.astype(bf),
        )
        back = back + d_hidden
        small_grads[layer] = (
            prenorm_grad,
            kernel_grad[:, :inner_local],
            offset_grad[:inner_local],
            kernel_grad[:, inner_local:],
            offset_grad[inner_local:],
            jnp.sum(g_step_raw, 0),
            g_decay * decay,
            skip_grad,
            norm_grad,
        )
    output = lax.dynamic_slice_in_dim(output, feat_start, feat, 1)
    back = lax.dynamic_slice_in_dim(back, feat_start, feat, 1)

    def stack_member(groups, member):
        return jnp.stack([groups[layer][member] for layer in range(layers)])

    members = [stack_member(small_grads, member) for member in range(9)]
    flat = jnp.concatenate([m.reshape(-1) for m in members])
    fill = -flat.shape[0] % 1024
    flat = jnp.concatenate([flat, jnp.zeros((fill,), jnp.float32)]).reshape(-1, 128)
    grads = [piece for layer in range(layers) for piece in shard_grads[layer]]
    gate_g, inner_g, extra_g, mixer_g, flat = reduce_grads(grads, flat)
    flat = flat.reshape(-1)
    summed, start = [], 0
    for m in members:
        summed.append(flat[start : start + m.size].reshape(m.shape))
        start += m.size
    return (
        output,
        back,
        summed[0],
        gate_g,
        inner_g,
        extra_g[:, :, : 2 * state_size],
        extra_g[:, :, 2 * state_size : 2 * state_size + heads_local],
        summed[1],
        summed[2],
        summed[3],
        summed[4],
        summed[5],
        summed[6],
        summed[7],
        summed[8],
        mixer_g,
    )


def pick(*args):
    nz, ny, n = (lax.axis_size(name) for name in ("fsdp", "ctx", "tp"))
    length, rows, cols = args[0].shape[0], args[4].shape[1], args[4].shape[2]
    heads, states = args[7].shape[2], args[6].shape[2]
    fits = ny == 2 and nz <= 4 and n > 1 and rows % 16 == 0 and cols % 128 == 0
    fits = fits and length % (16 * n) == 0 and length % 128 == 0 and cols >= states + heads
    return (body_kernels if fits else body)(*args)


def solution(mesh):
    placed = (
        P(("fsdp", "ctx"), None),
        P("fsdp", None),
        P(("fsdp", "ctx"), None),
        P(),
        P(None, ("fsdp", "ctx"), "tp"),
        P(None, ("fsdp", "ctx"), "tp"),
        P(None, ("fsdp", "ctx"), None),
        P(None, ("fsdp", "ctx"), "tp"),
        P(None, None, "tp"),
        P(None, "tp"),
        P(),
        P(),
        P(None, "tp"),
        P(None, "tp"),
        P(None, "tp"),
        P(None, "tp"),
        P(None, ("fsdp", "ctx"), "tp"),
    )
    return jax.shard_map(
        pick,
        mesh=mesh,
        in_specs=placed,
        out_specs=(
            P(("fsdp", "ctx"), "tp"),
            P(("fsdp", "ctx"), "tp"),
            P(None, "tp"),
            P(None, ("fsdp", "ctx"), "tp"),
            P(None, ("fsdp", "ctx"), "tp"),
            P(None, ("fsdp", "ctx"), None),
            P(None, ("fsdp", "ctx"), "tp"),
            P(None, None, "tp"),
            P(None, "tp"),
            P(),
            P(),
            P(None, "tp"),
            P(None, "tp"),
            P(None, "tp"),
            P(None, "tp"),
            P(None, ("fsdp", "ctx"), "tp"),
        ),
        check_vma=False,
    )
```

```python
import functools

import jax
import jax.numpy as jnp
from jax import lax
from jax.experimental import pallas as pl
from jax.experimental.pallas import tpu as pltpu
from jax.sharding import PartitionSpec as P

SPAN = 128


EPSILON = 1e-05
HIGH = lax.Precision.HIGHEST


def passed_along(block, axis, distance):
    devices = range(lax.axis_size(axis))
    route = [(i - distance, i) for i in devices if i - distance in devices]
    return lax.ppermute(block, axis, route)


def prefix(shard, axis, join, neutral):
    place = lax.axis_index(axis)
    gathered = jax.tree.map(
        lambda a, kind: lax.all_gather(a.astype(kind), axis), shard, (jnp.bfloat16, jnp.bfloat16)
    )
    state = jax.tree.map(lambda a, e: jnp.zeros_like(a) + jnp.asarray(e, a.dtype), shard, neutral)

    def prefix_one(turn, state):
        return join(
            state,
            jax.tree.map(
                lambda a, own: lax.dynamic_index_in_dim(a, turn, 0, False).astype(own.dtype),
                gathered,
                shard,
            ),
        )

    return lax.fori_loop(0, place, prefix_one, state)


def entering(shard, axis, join, neutral):
    count = lax.axis_size(axis)
    place = lax.axis_index(axis)
    ahead = count - 1 - place
    gathered = jax.tree.map(
        lambda a, kind: lax.all_gather(a.astype(kind), axis),
        shard,
        jax.tree.map(lambda a: jnp.bfloat16 if a.dtype == jnp.float32 else a.dtype, shard),
    )
    state = jax.tree.map(lambda a, e: jnp.zeros_like(a) + jnp.asarray(e, a.dtype), shard, neutral)

    def entering_one(turn, state):
        source = count - 1 - turn
        return join(
            state,
            jax.tree.map(
                lambda a, own: lax.dynamic_index_in_dim(a, source, 0, False).astype(own.dtype),
                gathered,
                shard,
            ),
        )

    return lax.fori_loop(0, ahead, entering_one, state)


def rms_apply(hidden, gain):
    inverse = lax.rsqrt(jnp.mean(hidden * hidden, axis=-1, keepdims=True) + EPSILON)
    return hidden * inverse * gain


def conv_apply(padded, seg_padded, kernel, offset):
    taps = kernel.shape[0]
    length = padded.shape[0] - taps + 1
    current = seg_padded[taps - 1 :]
    total = jnp.zeros((length, padded.shape[1]), jnp.float32) + offset
    for shift_index in range(taps):
        same = (seg_padded[shift_index : shift_index + length] == current).astype(jnp.float32)
        total = (
            total + kernel[shift_index] * padded[shift_index : shift_index + length] * same[:, None]
        )
    return jax.nn.silu(total)


def fresh_flags(seg, cont):
    first = jnp.reshape(1.0 - cont, (1,))
    return jnp.concatenate([first, (seg[1:] != seg[:-1]).astype(jnp.float32)])


def inflow(step, decay, seg, cont):
    alive = (jnp.cumsum(fresh_flags(seg, cont)) == 0.0).astype(jnp.float32)
    return alive[:, None] * jnp.exp(jnp.cumsum(step * decay[None, :], axis=0))


def ssd_block(inner, bmat, cmat, step, decay, skip, seg, cont, carry_in):
    length, heads, head_size = inner.shape
    blocks = length // SPAN
    fresh = fresh_flags(seg, cont)

    def advance(carry, piece):
        part_x, part_b, part_c, part_dt, part_seg, part_fresh = piece
        logs = jnp.cumsum(part_dt * decay[None, :], axis=0)
        order = jnp.arange(SPAN)
        allowed = (order[:, None] >= order[None, :]) & (part_seg[:, None] == part_seg[None, :])
        gap = logs[:, None, :] - logs[None, :, :]
        weights = jnp.where(
            allowed[:, :, None], jnp.exp(jnp.where(allowed[:, :, None], gap, 0.0)), 0.0
        )
        scores = jnp.dot(part_c, part_b.T, precision=HIGH)
        scaled = part_x * part_dt[:, :, None]
        local = jnp.einsum("tsh,shp->thp", weights * scores[:, :, None], scaled, precision=HIGH)
        alive = (jnp.cumsum(part_fresh) == 0.0).astype(jnp.float32)
        into = alive[:, None] * jnp.exp(logs)
        carried = into[:, :, None] * jnp.einsum("tn,hpn->thp", part_c, carry, precision=HIGH)
        tail = (
            jnp.exp(logs[-1][None, :] - logs)
            * (part_seg == part_seg[-1]).astype(jnp.float32)[:, None]
        )
        update = jnp.einsum("shp,sn->hpn", scaled * tail[:, :, None], part_b, precision=HIGH)
        return (into[-1][:, None, None] * carry + update, local + carried)

    pieces = (
        inner.reshape(blocks, SPAN, heads, head_size),
        bmat.reshape(blocks, SPAN, -1),
        cmat.reshape(blocks, SPAN, -1),
        step.reshape(blocks, SPAN, heads),
        seg.reshape(blocks, SPAN),
        fresh.reshape(blocks, SPAN),
    )
    final, outputs = lax.scan(advance, carry_in, pieces)
    return (outputs.reshape(length, heads, head_size) + skip[None, :, None] * inner, final)


def link(earlier, later):
    return (earlier[0] * later[0], later[0][:, None, None] * earlier[1] + later[1])


def contract_cols(left, right):
    return lax.dot_general(
        left, right, (((1,), (1,)), ((), ())), preferred_element_type=jnp.float32
    )


def project(normed, weight, feat_dim):
    return lax.dot_general(
        normed, weight, (((feat_dim,), (0,)), ((), ())), preferred_element_type=jnp.float32
    )


def grad_rows(normed, delta, feat_dim):
    return lax.dot_general(
        normed, delta, (((1 - feat_dim,), (0,)), ((), ())), preferred_element_type=jnp.float32
    )


MESH = pl.DeviceIdType.MESH
VM = pl.BlockSpec(memory_space=pltpu.VMEM)


def remote(src, dst, send, recv, where):
    return pltpu.make_async_remote_copy(
        src_ref=src, dst_ref=dst, send_sem=send, recv_sem=recv, device_id=where, device_id_type=MESH
    )


def greet(peers):
    barrier = pltpu.get_barrier_semaphore()
    for peer in peers:
        pl.semaphore_signal(barrier, inc=1, device_id=peer, device_id_type=MESH)
    pl.semaphore_wait(barrier, len(peers))


def weights_kernel(nz, ny, *refs):
    shards, (win, wmix), (own_sem, zsend, zrecv, ysend, yrecv) = refs[:4], refs[4:6], refs[6:]
    z, y = lax.axis_index("fsdp"), lax.axis_index("ctx")
    rows, cols = shards[0].shape[1:]
    z_at = lambda d: lax.rem(z + d, nz)
    y_at = lambda e: lax.rem(y + e, ny)
    greet([{"fsdp": z_at(d)} for d in range(1, nz)] + [{"ctx": y_at(e)} for e in range(1, ny)])

    def region(piece, zs, ys):
        at = pl.ds(pl.multiple_of((zs * ny + ys) * rows, rows), rows)
        if piece == 3:
            return wmix.at[:, at, :]
        return win.at[:, at, pl.ds(piece * cols, cols)]

    own, sends = [], []
    for piece in range(4):
        copy = pltpu.make_async_copy(shards[piece], region(piece, z, y), own_sem.at[piece])
        copy.start()
        own.append(copy)
    zcopies, ycopies = {}, {}
    for piece in range(4):
        for d in range(1, nz):
            copy = remote(
                shards[piece],
                region(piece, z, y),
                zsend.at[piece, d - 1],
                zrecv.at[piece, d - 1],
                {"fsdp": z_at(d)},
            )
            copy.start()
            zcopies[piece, d] = copy
        for e in range(1, ny):
            copy = remote(
                shards[piece],
                region(piece, z, y),
                ysend.at[piece, 0, e - 1],
                yrecv.at[piece, 0, e - 1],
                {"ctx": y_at(e)},
            )
            copy.start()
            ycopies[piece, 0, e] = copy
    for piece in range(4):
        for d in range(1, nz):
            zcopies[piece, d].wait_recv()
            block = region(piece, z_at(nz - d), y)
            for e in range(1, ny):
                copy = remote(
                    block,
                    block,
                    ysend.at[piece, d, e - 1],
                    yrecv.at[piece, d, e - 1],
                    {"ctx": y_at(e)},
                )
                copy.start()
                ycopies[piece, d, e] = copy
    for copy in own:
        copy.wait()
    for copy in zcopies.values():
        copy.wait_send()
    for copy in ycopies.values():
        copy.wait()


def gather_weights(gate, inner, extra, mixer):
    nz, ny = lax.axis_size("fsdp"), lax.axis_size("ctx")
    layers, rows, cols = gate.shape
    full = rows * nz * ny
    dma = pltpu.SemaphoreType.DMA
    return pl.pallas_call(
        functools.partial(weights_kernel, nz, ny),
        out_shape=(
            jax.ShapeDtypeStruct((layers, full, 3 * cols), gate.dtype),
            jax.ShapeDtypeStruct((layers, full, cols), gate.dtype),
        ),
        in_specs=[VM] * 4,
        out_specs=(VM, VM),
        scratch_shapes=[
            dma((4,)),
            dma((4, nz - 1)),
            dma((4, nz - 1)),
            dma((4, nz, ny - 1)),
            dma((4, nz, ny - 1)),
        ],
        compiler_params=pltpu.CompilerParams(collective_id=1, has_side_effects=True),
        name="weights",
    )(gate, inner, extra, mixer)


def grads_kernel(nz, layers, *refs):
    ins = refs[: 2 * layers]
    small = refs[2 * layers]
    outs = refs[2 * layers + 1 : 2 * layers + 5]
    small_out = refs[2 * layers + 5]
    rest = refs[2 * layers + 6 :]
    yin, ymix, pin, pmix, zin, zmix, srecv = rest[:7]
    ysend, yrecv, zsend, zrecv, ssend, srec, sown = rest[7:]
    ny = 2
    z, y = lax.axis_index("fsdp"), lax.axis_index("ctx")
    other = 1 - y
    rows, cols = outs[0].shape[1:]
    z_at = lambda d: lax.rem(z + d, nz)
    peers = []
    for d in range(nz):
        for where in (y, other):
            if not (d == 0 and where is y):
                peers.append({"fsdp": z_at(d), "ctx": where})
    greet(peers)
    me = z * ny + y
    keep = pltpu.make_async_copy(small, srecv.at[me], sown)
    keep.start()

    def chunk(zd, yd):
        return pl.ds(pl.multiple_of((zd * ny + yd) * rows, rows), rows)

    order = [(layer, d) for layer in range(layers) for d in list(range(1, nz)) + [0]]
    ycopies, zcopies, scopies = {}, {}, []
    for layer, d in order:
        at = chunk(z_at(d), other)
        for which, buffer in enumerate((yin, ymix)):
            copy = remote(
                ins[2 * layer + which].at[at, :],
                buffer.at[layer, d],
                ysend.at[layer, d, which],
                yrecv.at[layer, d, which],
                {"ctx": other},
            )
            copy.start()
            ycopies[layer, d, which] = copy
    for i, peer in enumerate(peers):
        copy = remote(small, srecv.at[me], ssend.at[i], srec.at[i], peer)
        copy.start()
        scopies.append(copy)
    for layer, d in order:
        at = chunk(z_at(d), y)
        for which, (got, put, land) in enumerate(((yin, pin, zin), (ymix, pmix, zmix))):
            ycopies[layer, d, which].wait_recv()
            total = ins[2 * layer + which][at, :].astype(jnp.float32) + got[layer, d].astype(
                jnp.float32
            )
            if d:
                put[layer, d - 1] = total.astype(jnp.bfloat16)
                copy = remote(
                    put.at[layer, d - 1],
                    land.at[layer, d - 1],
                    zsend.at[layer, d - 1, which],
                    zrecv.at[layer, d - 1, which],
                    {"fsdp": z_at(d)},
                )
                copy.start()
                zcopies[layer, d, which] = copy
            elif which:
                outs[3][layer] = total
            else:
                for part in range(3):
                    outs[part][layer] = total[:, part * cols : (part + 1) * cols]
    for layer in range(layers):
        for d in range(1, nz):
            zcopies[layer, d, 0].wait_recv()
            zcopies[layer, d, 1].wait_recv()
        for part in range(3):
            total = outs[part][layer]
            for d in range(1, nz):
                total = total + zin[layer, d - 1, :, part * cols : (part + 1) * cols].astype(
                    jnp.float32
                )
            outs[part][layer] = total
        total = outs[3][layer]
        for d in range(1, nz):
            total = total + zmix[layer, d - 1].astype(jnp.float32)
        outs[3][layer] = total
    keep.wait()
    for copy in scopies:
        copy.wait_recv()
    total = srecv[0]
    for i in range(1, nz * ny):
        total = total + srecv[i]
    small_out[...] = total
    for copy in list(ycopies.values()) + list(zcopies.values()) + scopies:
        copy.wait_send()


def reduce_grads(grads, small):
    nz = lax.axis_size("fsdp")
    layers = len(grads) // 2
    full, cols = grads[1].shape
    rows = full // (2 * nz)
    dma, bf = pltpu.SemaphoreType.DMA, jnp.bfloat16
    return pl.pallas_call(
        functools.partial(grads_kernel, nz, layers),
        out_shape=tuple(jax.ShapeDtypeStruct((layers, rows, cols), jnp.float32) for _ in range(4))
        + (jax.ShapeDtypeStruct(small.shape, jnp.float32),),
        in_specs=[VM] * (2 * layers + 1),
        out_specs=(VM,) * 5,
        scratch_shapes=[
            pltpu.VMEM((layers, nz, rows, 3 * cols), bf),
            pltpu.VMEM((layers, nz, rows, cols), bf),
            pltpu.VMEM((layers, nz - 1, rows, 3 * cols), bf),
            pltpu.VMEM((layers, nz - 1, rows, cols), bf),
            pltpu.VMEM((layers, nz - 1, rows, 3 * cols), bf),
            pltpu.VMEM((layers, nz - 1, rows, cols), bf),
            pltpu.VMEM((2 * nz,) + small.shape, jnp.float32),
            dma((layers, nz, 2)),
            dma((layers, nz, 2)),
            dma((layers, nz - 1, 2)),
            dma((layers, nz - 1, 2)),
            dma((2 * nz - 1,)),
            dma((2 * nz - 1,)),
            dma,
        ],
        compiler_params=pltpu.CompilerParams(collective_id=2, has_side_effects=True),
        name="grads",
    )(*grads, small)


def sum_kernel(n, tallied, *refs):
    if tallied:
        x, tally, out, tally_out, got, put, seen = refs[:7]
        send, recv, send2, recv2, tsend, trecv, town = refs[7:]
    else:
        x, out, got, put, send, recv, send2, recv2 = refs
    me = lax.axis_index("tp")
    rows = x.shape[0] // n
    at = lambda i: pl.ds(pl.multiple_of(i * rows, rows), rows)
    peers = [lax.rem(me + d, n) for d in range(1, n)]
    greet([{"tp": peer} for peer in peers])
    first, second, tallies = [], [], []
    for d, peer in enumerate(peers):
        copy = remote(x.at[at(peer), :], got.at[d], send.at[d], recv.at[d], {"tp": peer})
        copy.start()
        first.append(copy)
    if tallied:
        keep = pltpu.make_async_copy(tally, seen.at[me], town)
        keep.start()
        for d, peer in enumerate(peers):
            copy = remote(tally, seen.at[me], tsend.at[d], trecv.at[d], {"tp": peer})
            copy.start()
            tallies.append(copy)
    total = x[at(me), :].astype(jnp.float32)
    for d in range(n - 1):
        first[d].wait_recv()
        total = total + got[d].astype(jnp.float32)
    put[...] = total.astype(put.dtype)
    for d, peer in enumerate(peers):
        copy = remote(put, out.at[at(me), :], send2.at[d], recv2.at[d], {"tp": peer})
        copy.start()
        second.append(copy)
    out[at(me), :] = total.astype(put.dtype)
    if tallied:
        keep.wait()
        for copy in tallies:
            copy.wait_recv()
        total = seen[0]
        for i in range(1, n):
            total = total + seen[i]
        tally_out[...] = total
    for copy in second:
        copy.wait_recv()
    for copy in first + second + tallies:
        copy.wait_send()


def tp_sum(x, ident, tally=None):
    n = lax.axis_size("tp")
    rows, cols = x.shape
    dma = pltpu.SemaphoreType.DMA
    tallied = tally is not None
    block = pltpu.VMEM((n - 1, rows // n, cols), x.dtype)
    scratch = [block, pltpu.VMEM((rows // n, cols), x.dtype)]
    shape = jax.ShapeDtypeStruct(x.shape, x.dtype)
    if tallied:
        scratch.append(pltpu.VMEM((n,) + tally.shape, jnp.float32))
        shape = (shape, jax.ShapeDtypeStruct(tally.shape, jnp.float32))
    scratch += [dma((n - 1,))] * (6 if tallied else 4) + ([dma] if tallied else [])
    return pl.pallas_call(
        functools.partial(sum_kernel, n, tallied),
        out_shape=shape,
        in_specs=[VM] * (2 if tallied else 1),
        out_specs=(VM, VM) if tallied else VM,
        scratch_shapes=scratch,
        compiler_params=pltpu.CompilerParams(collective_id=ident, has_side_effects=True),
        name="tpsum",
    )(*((x, tally) if tallied else (x,)))


def dots(left, right, dims):
    return lax.dot_general(
        left, right, (dims, ((), ())), precision=HIGH, preferred_element_type=jnp.float32
    )


def scan_parts(x_ref, bc_ref, step_ref, sd_ref, sdt_ref, aux_ref, row_ref):
    length, width = x_ref.shape
    heads = step_ref.shape[1]
    size = width // heads
    states = bc_ref.shape[1] // 2
    order = lambda dim: lax.broadcasted_iota(jnp.int32, (length, length), dim)
    lower = order(0) >= order(1)
    upper = (order(0) <= order(1)).astype(jnp.float32)
    spread = (
        lax.broadcasted_iota(jnp.int32, (heads, width), 1) // size
        == lax.broadcasted_iota(jnp.int32, (heads, width), 0)
    ).astype(jnp.float32)
    rep = lambda v: dots(v, spread, ((1,), (0,)))
    logs = dots(lower.astype(jnp.float32), sd_ref[...], ((1,), (0,)))
    logs_row = dots(sdt_ref[...], upper, ((1,), (0,)))
    aux = aux_ref[...]
    allowed = lower & (aux[:, 0:1] == row_ref[...])
    into = aux[:, 1:2] * jnp.exp(logs)
    tail = jnp.exp(logs[length - 1 : length, :] - logs) * aux[:, 2:3]
    bmat, cmat = bc_ref[:, :states], bc_ref[:, states:]
    scores = dots(cmat, bmat, ((1,), (1,)))

    def weights(h):
        gap = logs[:, h : h + 1] - logs_row[h : h + 1, :]
        return jnp.where(allowed, jnp.exp(jnp.where(allowed, gap, 0.0)), 0.0)

    scaled = x_ref[...] * rep(step_ref[...])
    return heads, size, spread, rep, upper, into, tail, bmat, cmat, scores, weights, scaled


def scan_kernel(x_ref, bc_ref, step_ref, sd_ref, sdt_ref, aux_ref, row_ref, skip_ref, y_ref, made_ref, into_ref):
    heads, size, _, rep, _, into, tail, bmat, _, scores, weights, scaled = scan_parts(
        x_ref, bc_ref, step_ref, sd_ref, sdt_ref, aux_ref, row_ref
    )
    into_ref[...] = into
    made_ref[...] = dots(scaled * rep(tail), bmat, ((0,), (0,)))
    for h in range(heads):
        at = slice(h * size, (h + 1) * size)
        local = dots(weights(h) * scores, scaled[:, at], ((1,), (0,)))
        y_ref[:, at] = local + skip_ref[:, at] * x_ref[:, at]


def back_kernel(
    x_ref, bc_ref, step_ref, sd_ref, sdt_ref, aux_ref, row_ref, skip_ref, decay_ref, dm_ref,
    mixed_ref, enter_ref, leave_ref, dx_ref, dbc_ref, dstep_ref, ddecay_ref, dskip_ref, local_ref,
):
    heads, size, spread, rep, upper, into, tail, bmat, cmat, scores, weights, scaled = scan_parts(
        x_ref, bc_ref, step_ref, sd_ref, sdt_ref, aux_ref, row_ref
    )
    length, states = bmat.shape
    fold = lambda v: dots(v, spread, ((1,), (1,)))
    x, dm, enter, leave = x_ref[...], dm_ref[...], enter_ref[...], leave_ref[...]
    skip = skip_ref[...]
    tails = rep(tail)
    from_state = tails * dots(bmat, leave, ((1,), (1,)))
    d_scores = jnp.zeros((length, length), jnp.float32)
    for h in range(heads):
        at = slice(h * size, (h + 1) * size)
        weight = weights(h)
        dm_h = dm_ref[:, at]
        d_scores += weight * dots(dm_h, scaled[:, at], ((1,), (1,)))
        local_ref[:, at] = dots(weight * scores, dm_h, ((0,), (0,)))
    dbc_ref[:, :states] = dots(scaled * tails, leave, ((1,), (0,))) + dots(
        d_scores, cmat, ((0,), (0,))
    )
    dbc_ref[:, states:] = dots(dm * rep(into), enter, ((1,), (0,))) + dots(
        d_scores, bmat, ((1,), (0,))
    )
    d_scaled = local_ref[...] + from_state
    dx_ref[...] = d_scaled * rep(step_ref[...]) + skip * dm
    d_logs = fold(dm * (mixed_ref[...] - skip * x) - scaled * d_scaled)
    ones = jnp.ones((8, states), jnp.float32)
    passed = fold(dots(ones, enter * leave, ((1,), (1,))))[0:1, :]
    last = fold(jnp.sum(scaled * from_state, 0, keepdims=True))
    last = last + into[length - 1 : length, :] * passed
    rest = dots(upper, d_logs, ((1,), (0,))) + last
    dstep_ref[...] = fold(d_scaled * x) + rest * decay_ref[...]
    ddecay_ref[...] = jnp.sum(rest * step_ref[...], 0, keepdims=True)
    dskip_ref[...] = jnp.sum(dm * x, 0, keepdims=True)


def scan_forward(parts):
    length, width = parts[0].shape
    heads, states = parts[2].shape[1], parts[1].shape[1] // 2
    f32 = lambda *shape: jax.ShapeDtypeStruct(shape, jnp.float32)
    return pl.pallas_call(
        scan_kernel,
        out_shape=(f32(length, width), f32(width, states), f32(length, heads)),
        in_specs=[VM] * len(parts),
        out_specs=(VM,) * 3,
        name="scan_forward",
    )(*parts)


def scan_backward(parts):
    length, width = parts[0].shape
    heads, states = parts[2].shape[1], parts[1].shape[1] // 2
    f32 = lambda *shape: jax.ShapeDtypeStruct(shape, jnp.float32)
    return pl.pallas_call(
        back_kernel,
        out_shape=(
            f32(length, width), f32(length, 2 * states), f32(length, heads), f32(1, heads), f32(1, width),
        ),
        in_specs=[VM] * len(parts),
        out_specs=(VM,) * 5,
        scratch_shapes=[pltpu.VMEM((length, width), jnp.float32)],
        name="scan_backward",
    )(*parts)


def body(
    tokens,
    segments,
    cotangent,
    prenorm,
    gate_proj,
    inner_proj,
    state_proj,
    step_proj,
    inner_kernel,
    inner_offset,
    state_kernel,
    state_offset,
    step_bias,
    decay_log,
    skip_gain,
    norm_gain,
    mixer_out,
):
    length = tokens.shape[0]
    model = tokens.shape[1]
    layers = gate_proj.shape[0]
    taps = inner_kernel.shape[1]
    inner_local = gate_proj.shape[2]
    heads_local = step_proj.shape[2]
    head_size = inner_local // heads_local
    state_size = state_proj.shape[2] // 2
    inner_all = inner_local * lax.axis_size("tp")
    feat = model // lax.axis_size("tp")
    feat_start = lax.axis_index("tp") * feat
    start = lax.axis_index("ctx") * length
    seg_pad = jnp.concatenate([jnp.full((taps - 1,), -1, jnp.int32), segments[0]])
    seg_padded = lax.dynamic_slice_in_dim(seg_pad, start, length + taps - 1)
    seg_here = seg_padded[taps - 1 :]
    cont = (seg_padded[taps - 2] == seg_padded[taps - 1]).astype(jnp.float32)
    zeros_state = jnp.zeros((heads_local, head_size, state_size), jnp.float32)
    identity = (jnp.ones((heads_local,), jnp.float32), zeros_state)

    def layer_kernel(layer):
        kernel = jnp.concatenate([inner_kernel[layer], state_kernel[layer]], 1)
        offset = jnp.concatenate([inner_offset[layer], state_offset[layer]])
        return (kernel, offset)

    def split_act(act, layer):
        inner = act[:, :inner_local].reshape(length, heads_local, head_size)
        bmat = act[:, inner_local : inner_local + state_size]
        cmat = act[:, inner_local + state_size :]
        step = jax.nn.softplus(kept_step[layer] + step_bias[layer])
        return (inner, bmat, cmat, step)

    feat_dim = 1
    hidden = tokens.astype(jnp.float32)
    back = cotangent
    kept = []
    kept_step = []
    for layer in range(layers):
        mats = (
            lax.all_gather(gate_proj[layer], ("fsdp", "ctx"), axis=0, tiled=True),
            lax.all_gather(inner_proj[layer], ("fsdp", "ctx"), axis=0, tiled=True),
            lax.all_gather(state_proj[layer], ("fsdp", "ctx"), axis=0, tiled=True),
            lax.all_gather(step_proj[layer], ("fsdp", "ctx"), axis=0, tiled=True),
            lax.all_gather(mixer_out[layer], ("fsdp", "ctx"), axis=0, tiled=True),
        )
        gate_w, inner_w, state_w, step_w, mixer_w = mats
        inverse = None
        normed = rms_apply(hidden, prenorm[layer]).astype(jnp.bfloat16)
        gate = project(normed, gate_w, feat_dim)
        raw = jnp.concatenate(
            [
                project(normed, inner_w, feat_dim).astype(jnp.bfloat16),
                project(normed, state_w, feat_dim).astype(jnp.bfloat16),
            ],
            1,
        )
        step_raw = project(normed, step_w, feat_dim)
        kept_step.append(step_raw)
        before = passed_along(raw[length - (taps - 1) :], "ctx", 1)
        padded = jnp.concatenate([before, raw], 0).astype(jnp.float32)
        kernel, offset = layer_kernel(layer)
        act = conv_apply(padded, seg_padded, kernel, offset)
        inner, bmat, cmat, step = split_act(act, layer)
        decay = -jnp.exp(decay_log[layer])
        partial_mixed, produced = ssd_block(
            inner, bmat, cmat, step, decay, skip_gain[layer], seg_here, cont, zeros_state
        )
        flow = inflow(step, decay, seg_here, cont)
        incoming = prefix((flow[-1], produced), "ctx", link, identity)[1]
        mixed = partial_mixed + jnp.einsum("th,tn,hpn->thp", flow, cmat, incoming, precision=HIGH)
        mixed = mixed.reshape(length, inner_local)
        gated = mixed * jax.nn.silu(gate)
        squares = lax.psum(jnp.sum(gated * gated, 1), "tp")
        scale = lax.rsqrt(squares / inner_all + EPSILON)
        normout = (gated * scale[:, None] * norm_gain[layer]).astype(jnp.bfloat16)
        projected = lax.psum(contract_cols(normout, mixer_w), "tp")
        stored = None
        kept.append(
            (hidden, inverse, stored, normed, gate, padded, incoming, mixed, gated, scale, normout)
        )
        hidden = hidden + projected
    output = hidden
    shard_grads = [None] * layers
    small_grads = [None] * layers
    for layer in reversed(range(layers)):
        hidden_in, inverse, stored, normed, gate, padded, incoming, mixed, gated, scale, normout = (
            kept[layer]
        )
        mats = (
            lax.all_gather(gate_proj[layer], ("fsdp", "ctx"), axis=0, tiled=True),
            lax.all_gather(inner_proj[layer], ("fsdp", "ctx"), axis=0, tiled=True),
            lax.all_gather(state_proj[layer], ("fsdp", "ctx"), axis=0, tiled=True),
            lax.all_gather(step_proj[layer], ("fsdp", "ctx"), axis=0, tiled=True),
            lax.all_gather(mixer_out[layer], ("fsdp", "ctx"), axis=0, tiled=True),
        )
        gate_w, inner_w, state_w, step_w, mixer_w = mats
        gain = norm_gain[layer]
        back_b = back.astype(jnp.bfloat16)
        d_out = project(back_b, mixer_w, feat_dim)
        mixer_grad = grad_rows(back_b, normout, feat_dim)
        norm_grad = jnp.sum(d_out * gated * scale[:, None], 0)
        inner_total = lax.psum(jnp.sum(d_out * gain * gated, 1), "tp")
        d_gated = (
            scale[:, None] * gain * d_out - gated * (scale**3 * inner_total / inner_all)[:, None]
        )
        sigma = jax.nn.sigmoid(gate)
        d_mixed = d_gated * gate * sigma
        d_gate = (d_gated * mixed * sigma * (1.0 + gate * (1.0 - sigma))).astype(jnp.bfloat16)
        kernel, offset = layer_kernel(layer)
        act, conv_pull = jax.vjp(
            lambda pad, ker, off: conv_apply(pad, seg_padded, ker, off), padded, kernel, offset
        )
        inner, bmat, cmat, step = split_act(act, layer)
        decay = -jnp.exp(decay_log[layer])
        flow = inflow(step, decay, seg_here, cont)
        d_mixed3 = d_mixed.reshape(length, heads_local, head_size)
        adjoint = jnp.einsum("th,thp,tn->hpn", flow, d_mixed3, cmat, precision=HIGH)
        carried = entering((flow[-1], adjoint), "ctx", link, identity)[1]

        def mixer_local(inner_v, bmat_v, cmat_v, step_v, decay_v, skip_v, entry):
            part_v, produced_v = ssd_block(
                inner_v, bmat_v, cmat_v, step_v, decay_v, skip_v, seg_here, cont, zeros_state
            )
            flow_v = inflow(step_v, decay_v, seg_here, cont)
            result_v = part_v + jnp.einsum("th,tn,hpn->thp", flow_v, cmat_v, entry, precision=HIGH)
            return (result_v, flow_v[-1][:, None, None] * entry + produced_v)

        _, ssd_pull = jax.vjp(
            mixer_local, inner, bmat, cmat, step, decay, skip_gain[layer], incoming
        )
        g_inner, g_bmat, g_cmat, g_step, g_decay, skip_grad, _ = ssd_pull((d_mixed3, carried))
        g_state = lax.psum(jnp.concatenate([g_bmat, g_cmat], 1).astype(jnp.bfloat16), "tp").astype(
            jnp.float32
        )
        g_act = jnp.concatenate([g_inner.reshape(length, inner_local), g_state], 1)
        g_padded, kernel_grad, offset_grad = conv_pull(g_act)
        returned = passed_along(g_padded[: taps - 1], "ctx", -1)
        g_raw = g_padded[taps - 1 :] + jnp.concatenate(
            [jnp.zeros((length - (taps - 1), g_padded.shape[1]), jnp.float32), returned], 0
        )
        g_step_raw = g_step * jax.nn.sigmoid(kept_step[layer] + step_bias[layer])
        g_inner_b = g_raw[:, :inner_local].astype(jnp.bfloat16)
        g_state_b = g_raw[:, inner_local:].astype(jnp.bfloat16)
        g_step_b = g_step_raw.astype(jnp.bfloat16)
        partial_normed = (
            contract_cols(d_gate, gate_w)
            + contract_cols(g_inner_b, inner_w)
            + contract_cols(g_step_b, step_w)
        )
        d_normed = lax.psum(partial_normed.astype(jnp.bfloat16), "tp").astype(
            jnp.float32
        ) + contract_cols(g_state_b, state_w)
        _, norm_pull = jax.vjp(rms_apply, hidden_in, prenorm[layer])
        d_hidden, prenorm_full = norm_pull(d_normed)
        prenorm_grad = lax.dynamic_slice_in_dim(prenorm_full, feat_start, feat)
        shard_grads[layer] = (
            lax.psum_scatter(
                grad_rows(normed, d_gate, feat_dim),
                ("fsdp", "ctx"),
                scatter_dimension=0,
                tiled=True,
            ),
            lax.psum_scatter(
                grad_rows(normed, g_inner_b, feat_dim),
                ("fsdp", "ctx"),
                scatter_dimension=0,
                tiled=True,
            ),
            lax.psum_scatter(
                grad_rows(normed, g_state_b, feat_dim),
                ("fsdp", "ctx"),
                scatter_dimension=0,
                tiled=True,
            ),
            lax.psum_scatter(
                grad_rows(normed, g_step_b, feat_dim),
                ("fsdp", "ctx"),
                scatter_dimension=0,
                tiled=True,
            ),
            lax.psum_scatter(mixer_grad, ("fsdp", "ctx"), scatter_dimension=0, tiled=True),
        )
        back = back + d_hidden
        small_grads[layer] = (
            prenorm_grad,
            kernel_grad[:, :inner_local],
            offset_grad[:inner_local],
            kernel_grad[:, inner_local:],
            offset_grad[inner_local:],
            jnp.sum(g_step_raw, 0),
            g_decay * decay,
            skip_grad,
            norm_grad,
        )
    output = lax.dynamic_slice_in_dim(output, feat_start, feat, 1)
    back = lax.dynamic_slice_in_dim(back, feat_start, feat, 1)

    def stack_member(groups, member):
        return jnp.stack([groups[layer][member] for layer in range(layers)])

    summed = lax.psum(
        (
            stack_member(small_grads, 0),
            stack_member(small_grads, 1),
            stack_member(small_grads, 2),
            stack_member(small_grads, 3),
            stack_member(small_grads, 4),
            stack_member(small_grads, 5),
            stack_member(small_grads, 6),
            stack_member(small_grads, 7),
            stack_member(small_grads, 8),
        ),
        ("fsdp", "ctx"),
    )
    return (
        output,
        back,
        summed[0],
        stack_member(shard_grads, 0),
        stack_member(shard_grads, 1),
        stack_member(shard_grads, 2),
        stack_member(shard_grads, 3),
        summed[1],
        summed[2],
        summed[3],
        summed[4],
        summed[5],
        summed[6],
        summed[7],
        summed[8],
        stack_member(shard_grads, 4),
    )


def contract_high(left, right, left_dim, right_dim):
    return lax.dot_general(
        left, right, (((left_dim,), (right_dim,)), ((), ())), precision=HIGH
    )


def body_kernels(
    tokens,
    segments,
    cotangent,
    prenorm,
    gate_proj,
    inner_proj,
    state_proj,
    step_proj,
    inner_kernel,
    inner_offset,
    state_kernel,
    state_offset,
    step_bias,
    decay_log,
    skip_gain,
    norm_gain,
    mixer_out,
):
    length = tokens.shape[0]
    model = tokens.shape[1]
    layers = gate_proj.shape[0]
    taps = inner_kernel.shape[1]
    inner_local = gate_proj.shape[2]
    heads_local = step_proj.shape[2]
    head_size = inner_local // heads_local
    state_size = state_proj.shape[2] // 2
    inner_all = inner_local * lax.axis_size("tp")
    feat = model // lax.axis_size("tp")
    feat_start = lax.axis_index("tp") * feat
    start = lax.axis_index("ctx") * length
    seg_pad = jnp.concatenate([jnp.full((taps - 1,), -1, jnp.int32), segments[0]])
    seg_padded = lax.dynamic_slice_in_dim(seg_pad, start, length + taps - 1)
    seg_here = seg_padded[taps - 1 :]
    cont = (seg_padded[taps - 2] == seg_padded[taps - 1]).astype(jnp.float32)
    zeros_state = jnp.zeros((heads_local, head_size, state_size), jnp.float32)
    identity = (jnp.ones((heads_local,), jnp.float32), zeros_state)

    def layer_kernel(layer):
        kernel = jnp.concatenate([inner_kernel[layer], state_kernel[layer]], 1)
        offset = jnp.concatenate([inner_offset[layer], state_offset[layer]])
        return (kernel, offset)

    def split_act(act, layer):
        inner = act[:, :inner_local].reshape(length, heads_local, head_size)
        bmat = act[:, inner_local : inner_local + state_size]
        cmat = act[:, inner_local + state_size :]
        step = jax.nn.softplus(kept_step[layer] + step_bias[layer])
        return (inner, bmat, cmat, step)

    feat_dim = 1
    hidden = tokens.astype(jnp.float32)
    back = cotangent
    kept = []
    kept_step = []
    cols = inner_local
    pad = cols - 2 * state_size - heads_local
    extra = jnp.concatenate(
        [state_proj, step_proj, jnp.zeros(step_proj.shape[:2] + (pad,), step_proj.dtype)], 2
    )
    win, wmix = gather_weights(gate_proj, inner_proj, extra, mixer_out)
    bf = jnp.bfloat16
    fresh = fresh_flags(seg_here, cont)
    aux = jnp.stack(
        [
            seg_here.astype(jnp.float32),
            (jnp.cumsum(fresh) == 0.0).astype(jnp.float32),
            (seg_here == seg_here[-1]).astype(jnp.float32),
        ],
        1,
    )
    seg_row = seg_here.astype(jnp.float32)[None]
    lead = (lax.axis_index("tp") == 0).astype(bf)
    for layer in range(layers):
        inverse = None
        normed = rms_apply(hidden, prenorm[layer]).astype(jnp.bfloat16)
        wide = project(normed, win[layer], feat_dim)
        gate = wide[:, :cols]
        raw = wide[:, cols : 2 * cols + 2 * state_size].astype(bf)
        step_raw = wide[:, 2 * cols + 2 * state_size :][:, :heads_local]
        kept_step.append(step_raw)
        before = passed_along(raw[length - (taps - 1) :], "ctx", 1)
        padded = jnp.concatenate([before, raw], 0).astype(jnp.float32)
        kernel, offset = layer_kernel(layer)
        act = conv_apply(padded, seg_padded, kernel, offset)
        decay = -jnp.exp(decay_log[layer])
        step = jax.nn.softplus(step_raw + step_bias[layer])
        marks = step * decay
        parts = (
            act[:, :inner_local],
            act[:, inner_local:],
            step,
            marks,
            marks.T,
            aux,
            seg_row,
            jnp.repeat(skip_gain[layer], head_size)[None],
        )
        partial_mixed, produced, flow = scan_forward(parts)
        incoming = passed_along(produced.astype(bf), "ctx", 1).astype(jnp.float32)
        reach = contract_high(act[:, inner_local + state_size :], incoming, 1, 1)
        mixed = partial_mixed + jnp.repeat(flow, head_size, axis=1) * reach
        gated = mixed * jax.nn.silu(gate)
        squares = jnp.broadcast_to(jnp.sum(gated * gated, 1)[None], (8, length))
        lifted = (gated * norm_gain[layer]).astype(bf)
        projected, squares = tp_sum(contract_cols(lifted, wmix[layer]).astype(bf), 3, squares)
        projected = projected.astype(jnp.float32)
        scale = lax.rsqrt(squares[0] / inner_all + EPSILON)
        normout = (gated * scale[:, None] * norm_gain[layer]).astype(bf)
        stored = projected
        kept.append(
            (hidden, (parts, flow, decay), stored, normed, gate, padded, incoming, mixed, gated, scale, normout)
        )
        hidden = hidden + projected * scale[:, None]
    output = hidden
    shard_grads = [None] * layers
    small_grads = [None] * layers
    for layer in reversed(range(layers)):
        hidden_in, inverse, stored, normed, gate, padded, incoming, mixed, gated, scale, normout = (
            kept[layer]
        )
        gain = norm_gain[layer]
        back_b = back.astype(jnp.bfloat16)
        d_out = project(back_b, wmix[layer], feat_dim)
        mixer_grad = grad_rows(back_b, normout, feat_dim)
        norm_grad = jnp.sum(d_out * gated * scale[:, None], 0)
        inner_total = jnp.sum(back_b.astype(jnp.float32) * stored, 1)
        d_gated = (
            scale[:, None] * gain * d_out - gated * (scale**3 * inner_total / inner_all)[:, None]
        )
        sigma = jax.nn.sigmoid(gate)
        d_mixed = d_gated * gate * sigma
        d_gate = (d_gated * mixed * sigma * (1.0 + gate * (1.0 - sigma))).astype(jnp.bfloat16)
        kernel, offset = layer_kernel(layer)
        parts, flow, decay = inverse
        _, conv_pull = jax.vjp(
            lambda pad, ker, off: conv_apply(pad, seg_padded, ker, off), padded, kernel, offset
        )
        cmat = parts[1][:, state_size:]
        adjoint = contract_high(jnp.repeat(flow, head_size, axis=1) * d_mixed, cmat, 0, 0)
        carried = passed_along(adjoint.astype(bf), "ctx", -1).astype(jnp.float32)
        g_inner, g_both, g_step, g_decay, skip_grad = scan_backward(
            parts + (decay[None], d_mixed, mixed, incoming, carried)
        )
        g_decay = g_decay[0]
        skip_grad = jnp.sum(skip_grad.reshape(heads_local, head_size), 1)
        g_state = tp_sum(g_both.astype(bf), 4).astype(jnp.float32)
        g_act = jnp.concatenate([g_inner.reshape(length, inner_local), g_state], 1)
        g_padded, kernel_grad, offset_grad = conv_pull(g_act)
        returned = passed_along(g_padded[: taps - 1], "ctx", -1)
        g_raw = g_padded[taps - 1 :] + jnp.concatenate(
            [jnp.zeros((length - (taps - 1), g_padded.shape[1]), jnp.float32), returned], 0
        )
        g_step_raw = g_step * jax.nn.sigmoid(kept_step[layer] + step_bias[layer])
        g_inner_b = g_raw[:, :inner_local].astype(jnp.bfloat16)
        g_state_b = g_raw[:, inner_local:].astype(jnp.bfloat16)
        g_step_b = g_step_raw.astype(jnp.bfloat16)
        blank = jnp.zeros((length, pad), bf)
        delta = jnp.concatenate([d_gate, g_inner_b, g_state_b, g_step_b, blank], 1)
        single = jnp.concatenate([d_gate, g_inner_b, g_state_b * lead, g_step_b, blank], 1)
        d_normed = tp_sum(contract_cols(single, win[layer]).astype(bf), 5).astype(jnp.float32)
        _, norm_pull = jax.vjp(rms_apply, hidden_in, prenorm[layer])
        d_hidden, prenorm_full = norm_pull(d_normed)
        prenorm_grad = lax.dynamic_slice_in_dim(prenorm_full, feat_start, feat)
        shard_grads[layer] = (
            grad_rows(normed, delta, feat_dim).astype(bf),
            mixer_grad.astype(bf),
        )
        back = back + d_hidden
        small_grads[layer] = (
            prenorm_grad,
            kernel_grad[:, :inner_local],
            offset_grad[:inner_local],
            kernel_grad[:, inner_local:],
            offset_grad[inner_local:],
            jnp.sum(g_step_raw, 0),
            g_decay * decay,
            skip_grad,
            norm_grad,
        )
    output = lax.dynamic_slice_in_dim(output, feat_start, feat, 1)
    back = lax.dynamic_slice_in_dim(back, feat_start, feat, 1)

    def stack_member(groups, member):
        return jnp.stack([groups[layer][member] for layer in range(layers)])

    members = [stack_member(small_grads, member) for member in range(9)]
    flat = jnp.concatenate([m.reshape(-1) for m in members])
    fill = -flat.shape[0] % 1024
    flat = jnp.concatenate([flat, jnp.zeros((fill,), jnp.float32)]).reshape(-1, 128)
    grads = [piece for layer in range(layers) for piece in shard_grads[layer]]
    gate_g, inner_g, extra_g, mixer_g, flat = reduce_grads(grads, flat)
    flat = flat.reshape(-1)
    summed, start = [], 0
    for m in members:
        summed.append(flat[start : start + m.size].reshape(m.shape))
        start += m.size
    return (
        output,
        back,
        summed[0],
        gate_g,
        inner_g,
        extra_g[:, :, : 2 * state_size],
        extra_g[:, :, 2 * state_size : 2 * state_size + heads_local],
        summed[1],
        summed[2],
        summed[3],
        summed[4],
        summed[5],
        summed[6],
        summed[7],
        summed[8],
        mixer_g,
    )


def pick(*args):
    nz, ny, n = (lax.axis_size(name) for name in ("fsdp", "ctx", "tp"))
    length, rows, cols = args[0].shape[0], args[4].shape[1], args[4].shape[2]
    heads, states = args[7].shape[2], args[6].shape[2]
    fits = ny == 2 and nz <= 4 and n > 1 and rows % 16 == 0 and cols % 128 == 0
    fits = fits and length % (16 * n) == 0 and length == SPAN and cols >= states + heads
    return (body_kernels if fits else body)(*args)


def solution(mesh):
    placed = (
        P(("fsdp", "ctx"), None),
        P("fsdp", None),
        P(("fsdp", "ctx"), None),
        P(),
        P(None, ("fsdp", "ctx"), "tp"),
        P(None, ("fsdp", "ctx"), "tp"),
        P(None, ("fsdp", "ctx"), None),
        P(None, ("fsdp", "ctx"), "tp"),
        P(None, None, "tp"),
        P(None, "tp"),
        P(),
        P(),
        P(None, "tp"),
        P(None, "tp"),
        P(None, "tp"),
        P(None, "tp"),
        P(None, ("fsdp", "ctx"), "tp"),
    )
    return jax.shard_map(
        pick,
        mesh=mesh,
        in_specs=placed,
        out_specs=(
            P(("fsdp", "ctx"), "tp"),
            P(("fsdp", "ctx"), "tp"),
            P(None, "tp"),
            P(None, ("fsdp", "ctx"), "tp"),
            P(None, ("fsdp", "ctx"), "tp"),
            P(None, ("fsdp", "ctx"), None),
            P(None, ("fsdp", "ctx"), "tp"),
            P(None, None, "tp"),
            P(None, "tp"),
            P(),
            P(),
            P(None, "tp"),
            P(None, "tp"),
            P(None, "tp"),
            P(None, "tp"),
            P(None, ("fsdp", "ctx"), "tp"),
        ),
        check_vma=False,
    )
```

```python
import functools

import jax
import jax.numpy as jnp
from jax import lax
from jax.experimental import pallas as pl
from jax.experimental.pallas import tpu as pltpu
from jax.sharding import PartitionSpec as P

SPAN = 128


EPSILON = 1e-05
HIGH = lax.Precision.HIGHEST


def passed_along(block, axis, distance):
    devices = range(lax.axis_size(axis))
    route = [(i - distance, i) for i in devices if i - distance in devices]
    return lax.ppermute(block, axis, route)


def prefix(shard, axis, join, neutral):
    place = lax.axis_index(axis)
    gathered = jax.tree.map(
        lambda a, kind: lax.all_gather(a.astype(kind), axis), shard, (jnp.bfloat16, jnp.bfloat16)
    )
    state = jax.tree.map(lambda a, e: jnp.zeros_like(a) + jnp.asarray(e, a.dtype), shard, neutral)

    def prefix_one(turn, state):
        return join(
            state,
            jax.tree.map(
                lambda a, own: lax.dynamic_index_in_dim(a, turn, 0, False).astype(own.dtype),
                gathered,
                shard,
            ),
        )

    return lax.fori_loop(0, place, prefix_one, state)


def entering(shard, axis, join, neutral):
    count = lax.axis_size(axis)
    place = lax.axis_index(axis)
    ahead = count - 1 - place
    gathered = jax.tree.map(
        lambda a, kind: lax.all_gather(a.astype(kind), axis),
        shard,
        jax.tree.map(lambda a: jnp.bfloat16 if a.dtype == jnp.float32 else a.dtype, shard),
    )
    state = jax.tree.map(lambda a, e: jnp.zeros_like(a) + jnp.asarray(e, a.dtype), shard, neutral)

    def entering_one(turn, state):
        source = count - 1 - turn
        return join(
            state,
            jax.tree.map(
                lambda a, own: lax.dynamic_index_in_dim(a, source, 0, False).astype(own.dtype),
                gathered,
                shard,
            ),
        )

    return lax.fori_loop(0, ahead, entering_one, state)


def rms_apply(hidden, gain):
    inverse = lax.rsqrt(jnp.mean(hidden * hidden, axis=-1, keepdims=True) + EPSILON)
    return hidden * inverse * gain


def conv_apply(padded, seg_padded, kernel, offset):
    taps = kernel.shape[0]
    length = padded.shape[0] - taps + 1
    current = seg_padded[taps - 1 :]
    total = jnp.zeros((length, padded.shape[1]), jnp.float32) + offset
    for shift_index in range(taps):
        same = (seg_padded[shift_index : shift_index + length] == current).astype(jnp.float32)
        total = (
            total + kernel[shift_index] * padded[shift_index : shift_index + length] * same[:, None]
        )
    return jax.nn.silu(total)


def fresh_flags(seg, cont):
    first = jnp.reshape(1.0 - cont, (1,))
    return jnp.concatenate([first, (seg[1:] != seg[:-1]).astype(jnp.float32)])


def inflow(step, decay, seg, cont):
    alive = (jnp.cumsum(fresh_flags(seg, cont)) == 0.0).astype(jnp.float32)
    return alive[:, None] * jnp.exp(jnp.cumsum(step * decay[None, :], axis=0))


def ssd_block(inner, bmat, cmat, step, decay, skip, seg, cont, carry_in):
    length, heads, head_size = inner.shape
    blocks = length // SPAN
    fresh = fresh_flags(seg, cont)

    def advance(carry, piece):
        part_x, part_b, part_c, part_dt, part_seg, part_fresh = piece
        logs = jnp.cumsum(part_dt * decay[None, :], axis=0)
        order = jnp.arange(SPAN)
        allowed = (order[:, None] >= order[None, :]) & (part_seg[:, None] == part_seg[None, :])
        gap = logs[:, None, :] - logs[None, :, :]
        weights = jnp.where(
            allowed[:, :, None], jnp.exp(jnp.where(allowed[:, :, None], gap, 0.0)), 0.0
        )
        scores = jnp.dot(part_c, part_b.T, precision=HIGH)
        scaled = part_x * part_dt[:, :, None]
        local = jnp.einsum("tsh,shp->thp", weights * scores[:, :, None], scaled, precision=HIGH)
        alive = (jnp.cumsum(part_fresh) == 0.0).astype(jnp.float32)
        into = alive[:, None] * jnp.exp(logs)
        carried = into[:, :, None] * jnp.einsum("tn,hpn->thp", part_c, carry, precision=HIGH)
        tail = (
            jnp.exp(logs[-1][None, :] - logs)
            * (part_seg == part_seg[-1]).astype(jnp.float32)[:, None]
        )
        update = jnp.einsum("shp,sn->hpn", scaled * tail[:, :, None], part_b, precision=HIGH)
        return (into[-1][:, None, None] * carry + update, local + carried)

    pieces = (
        inner.reshape(blocks, SPAN, heads, head_size),
        bmat.reshape(blocks, SPAN, -1),
        cmat.reshape(blocks, SPAN, -1),
        step.reshape(blocks, SPAN, heads),
        seg.reshape(blocks, SPAN),
        fresh.reshape(blocks, SPAN),
    )
    final, outputs = lax.scan(advance, carry_in, pieces)
    return (outputs.reshape(length, heads, head_size) + skip[None, :, None] * inner, final)


def link(earlier, later):
    return (earlier[0] * later[0], later[0][:, None, None] * earlier[1] + later[1])


def contract_cols(left, right):
    return lax.dot_general(
        left, right, (((1,), (1,)), ((), ())), preferred_element_type=jnp.float32
    )


def project(normed, weight, feat_dim):
    return lax.dot_general(
        normed, weight, (((feat_dim,), (0,)), ((), ())), preferred_element_type=jnp.float32
    )


def grad_rows(normed, delta, feat_dim):
    return lax.dot_general(
        normed, delta, (((1 - feat_dim,), (0,)), ((), ())), preferred_element_type=jnp.float32
    )


MESH = pl.DeviceIdType.MESH
VM = pl.BlockSpec(memory_space=pltpu.VMEM)


def remote(src, dst, send, recv, where):
    return pltpu.make_async_remote_copy(
        src_ref=src, dst_ref=dst, send_sem=send, recv_sem=recv, device_id=where, device_id_type=MESH
    )


def greet(peers):
    barrier = pltpu.get_barrier_semaphore()
    for peer in peers:
        pl.semaphore_signal(barrier, inc=1, device_id=peer, device_id_type=MESH)
    pl.semaphore_wait(barrier, len(peers))


def weights_kernel(nz, ny, *refs):
    shards, (win, wmix), (own_sem, zsend, zrecv, ysend, yrecv) = refs[:4], refs[4:6], refs[6:]
    z, y = lax.axis_index("fsdp"), lax.axis_index("ctx")
    rows, cols = shards[0].shape[1:]
    z_at = lambda d: lax.rem(z + d, nz)
    y_at = lambda e: lax.rem(y + e, ny)
    greet([{"fsdp": z_at(d)} for d in range(1, nz)] + [{"ctx": y_at(e)} for e in range(1, ny)])

    def region(piece, zs, ys):
        at = pl.ds(pl.multiple_of((zs * ny + ys) * rows, rows), rows)
        if piece == 3:
            return wmix.at[:, at, :]
        return win.at[:, at, pl.ds(piece * cols, cols)]

    own, sends = [], []
    for piece in range(4):
        copy = pltpu.make_async_copy(shards[piece], region(piece, z, y), own_sem.at[piece])
        copy.start()
        own.append(copy)
    zcopies, ycopies = {}, {}
    for piece in range(4):
        for d in range(1, nz):
            copy = remote(
                shards[piece],
                region(piece, z, y),
                zsend.at[piece, d - 1],
                zrecv.at[piece, d - 1],
                {"fsdp": z_at(d)},
            )
            copy.start()
            zcopies[piece, d] = copy
        for e in range(1, ny):
            copy = remote(
                shards[piece],
                region(piece, z, y),
                ysend.at[piece, 0, e - 1],
                yrecv.at[piece, 0, e - 1],
                {"ctx": y_at(e)},
            )
            copy.start()
            ycopies[piece, 0, e] = copy
    for piece in range(4):
        for d in range(1, nz):
            zcopies[piece, d].wait_recv()
            block = region(piece, z_at(nz - d), y)
            for e in range(1, ny):
                copy = remote(
                    block,
                    block,
                    ysend.at[piece, d, e - 1],
                    yrecv.at[piece, d, e - 1],
                    {"ctx": y_at(e)},
                )
                copy.start()
                ycopies[piece, d, e] = copy
    for copy in own:
        copy.wait()
    for copy in zcopies.values():
        copy.wait_send()
    for copy in ycopies.values():
        copy.wait()


def gather_weights(gate, inner, extra, mixer):
    nz, ny = lax.axis_size("fsdp"), lax.axis_size("ctx")
    layers, rows, cols = gate.shape
    full = rows * nz * ny
    dma = pltpu.SemaphoreType.DMA
    return pl.pallas_call(
        functools.partial(weights_kernel, nz, ny),
        out_shape=(
            jax.ShapeDtypeStruct((layers, full, 3 * cols), gate.dtype),
            jax.ShapeDtypeStruct((layers, full, cols), gate.dtype),
        ),
        in_specs=[VM] * 4,
        out_specs=(VM, VM),
        scratch_shapes=[
            dma((4,)),
            dma((4, nz - 1)),
            dma((4, nz - 1)),
            dma((4, nz, ny - 1)),
            dma((4, nz, ny - 1)),
        ],
        compiler_params=pltpu.CompilerParams(collective_id=1, has_side_effects=True),
        name="weights",
    )(gate, inner, extra, mixer)


def grads_kernel(nz, layers, *refs):
    ins = refs[: 2 * layers]
    small = refs[2 * layers]
    outs = refs[2 * layers + 1 : 2 * layers + 5]
    step_out = refs[2 * layers + 5]
    small_outs = refs[2 * layers + 6 : 2 * layers + 15]
    rest = refs[2 * layers + 15 :]
    extra, = rest[-1:]
    wide, heads = outs[2].shape[2], step_out.shape[2]
    outs = (outs[0], outs[1], extra, outs[3])
    state_out = refs[2 * layers + 3]
    yin, ymix, pin, pmix, zin, zmix, srecv = rest[:7]
    ysend, yrecv, zsend, zrecv, ssend, srec, sown = rest[7:-1]
    ny = 2
    z, y = lax.axis_index("fsdp"), lax.axis_index("ctx")
    other = 1 - y
    rows, cols = outs[0].shape[1:]
    z_at = lambda d: lax.rem(z + d, nz)
    peers = []
    for d in range(nz):
        for where in (y, other):
            if not (d == 0 and where is y):
                peers.append({"fsdp": z_at(d), "ctx": where})
    greet(peers)
    me = z * ny + y
    keep = pltpu.make_async_copy(small, srecv.at[me], sown)
    keep.start()

    def chunk(zd, yd):
        return pl.ds(pl.multiple_of((zd * ny + yd) * rows, rows), rows)

    order = [(layer, d) for layer in range(layers) for d in list(range(1, nz)) + [0]]
    ycopies, zcopies, scopies = {}, {}, []
    for layer, d in order:
        at = chunk(z_at(d), other)
        for which, buffer in enumerate((yin, ymix)):
            copy = remote(
                ins[2 * layer + which].at[at, :],
                buffer.at[layer, d],
                ysend.at[layer, d, which],
                yrecv.at[layer, d, which],
                {"ctx": other},
            )
            copy.start()
            ycopies[layer, d, which] = copy
    for i, peer in enumerate(peers):
        copy = remote(small, srecv.at[me], ssend.at[i], srec.at[i], peer)
        copy.start()
        scopies.append(copy)
    for layer, d in order:
        at = chunk(z_at(d), y)
        for which, (got, put, land) in enumerate(((yin, pin, zin), (ymix, pmix, zmix))):
            ycopies[layer, d, which].wait_recv()
            total = ins[2 * layer + which][at, :].astype(jnp.float32) + got[layer, d].astype(
                jnp.float32
            )
            if d:
                put[layer, d - 1] = total.astype(jnp.bfloat16)
                copy = remote(
                    put.at[layer, d - 1],
                    land.at[layer, d - 1],
                    zsend.at[layer, d - 1, which],
                    zrecv.at[layer, d - 1, which],
                    {"fsdp": z_at(d)},
                )
                copy.start()
                zcopies[layer, d, which] = copy
            elif which:
                outs[3][layer] = total
            else:
                for part in range(3):
                    outs[part][layer] = total[:, part * cols : (part + 1) * cols]
    for layer in range(layers):
        for d in range(1, nz):
            zcopies[layer, d, 0].wait_recv()
            zcopies[layer, d, 1].wait_recv()
        for part in range(3):
            total = outs[part][layer]
            for d in range(1, nz):
                total = total + zin[layer, d - 1, :, part * cols : (part + 1) * cols].astype(
                    jnp.float32
                )
            outs[part][layer] = total
        total = outs[3][layer]
        for d in range(1, nz):
            total = total + zmix[layer, d - 1].astype(jnp.float32)
        outs[3][layer] = total
    state_out[...] = extra[:, :, :wide]
    step_out[...] = extra[:, :, wide : wide + heads]
    keep.wait()
    for copy in scopies:
        copy.wait_recv()
    total = srecv[0]
    for i in range(1, nz * ny):
        total = total + srecv[i]
    start = 0
    for out in small_outs:
        width = out.shape[-1]
        if len(out.shape) == 2:
            out[...] = total[start : start + layers, :width]
            start += layers
        else:
            for layer in range(layers):
                out[layer] = total[start : start + out.shape[1], :width]
                start += out.shape[1]
    for copy in list(ycopies.values()) + list(zcopies.values()) + scopies:
        copy.wait_send()


def reduce_grads(grads, small, shapes, wide, heads):
    nz = lax.axis_size("fsdp")
    layers = len(grads) // 2
    full, cols = grads[1].shape
    rows = full // (2 * nz)
    dma, bf = pltpu.SemaphoreType.DMA, jnp.bfloat16
    return pl.pallas_call(
        functools.partial(grads_kernel, nz, layers),
        out_shape=tuple(
            jax.ShapeDtypeStruct(shape, jnp.float32)
            for shape in [(layers, rows, width) for width in (cols, cols, wide, cols, heads)] + shapes
        ),
        in_specs=[VM] * (2 * layers + 1),
        out_specs=(VM,) * (5 + len(shapes)),
        scratch_shapes=[
            pltpu.VMEM((layers, nz, rows, 3 * cols), bf),
            pltpu.VMEM((layers, nz, rows, cols), bf),
            pltpu.VMEM((layers, nz - 1, rows, 3 * cols), bf),
            pltpu.VMEM((layers, nz - 1, rows, cols), bf),
            pltpu.VMEM((layers, nz - 1, rows, 3 * cols), bf),
            pltpu.VMEM((layers, nz - 1, rows, cols), bf),
            pltpu.VMEM((2 * nz,) + small.shape, jnp.float32),
            dma((layers, nz, 2)),
            dma((layers, nz, 2)),
            dma((layers, nz - 1, 2)),
            dma((layers, nz - 1, 2)),
            dma((2 * nz - 1,)),
            dma((2 * nz - 1,)),
            dma,
            pltpu.VMEM((layers, rows, cols), jnp.float32),
        ],
        compiler_params=pltpu.CompilerParams(collective_id=2, has_side_effects=True),
        name="grads",
    )(*grads, small)


def sum_kernel(n, tallied, *refs):
    if tallied:
        x, tally, out, tally_out, got, put, seen = refs[:7]
        send, recv, send2, recv2, tsend, trecv, town = refs[7:]
    else:
        x, out, got, put, send, recv, send2, recv2 = refs
    me = lax.axis_index("tp")
    rows = x.shape[0] // n
    at = lambda i: pl.ds(pl.multiple_of(i * rows, rows), rows)
    peers = [lax.rem(me + d, n) for d in range(1, n)]
    greet([{"tp": peer} for peer in peers])
    first, second, tallies = [], [], []
    for d, peer in enumerate(peers):
        copy = remote(x.at[at(peer), :], got.at[d], send.at[d], recv.at[d], {"tp": peer})
        copy.start()
        first.append(copy)
    if tallied:
        keep = pltpu.make_async_copy(tally, seen.at[me], town)
        keep.start()
        for d, peer in enumerate(peers):
            copy = remote(tally, seen.at[me], tsend.at[d], trecv.at[d], {"tp": peer})
            copy.start()
            tallies.append(copy)
    total = x[at(me), :].astype(jnp.float32)
    for d in range(n - 1):
        first[d].wait_recv()
        total = total + got[d].astype(jnp.float32)
    put[...] = total.astype(put.dtype)
    for d, peer in enumerate(peers):
        copy = remote(put, out.at[at(me), :], send2.at[d], recv2.at[d], {"tp": peer})
        copy.start()
        second.append(copy)
    out[at(me), :] = total.astype(put.dtype)
    if tallied:
        keep.wait()
        for copy in tallies:
            copy.wait_recv()
        total = seen[0]
        for i in range(1, n):
            total = total + seen[i]
        tally_out[...] = total
    for copy in second:
        copy.wait_recv()
    for copy in first + second + tallies:
        copy.wait_send()


def share_kernel(n, x, out, seen, send, recv, own):
    me = lax.axis_index("tp")
    peers = [lax.rem(me + d, n) for d in range(1, n)]
    greet([{"tp": peer} for peer in peers])
    keep = pltpu.make_async_copy(x, seen.at[me], own)
    keep.start()
    copies = []
    for d, peer in enumerate(peers):
        copy = remote(x, seen.at[me], send.at[d], recv.at[d], {"tp": peer})
        copy.start()
        copies.append(copy)
    keep.wait()
    for copy in copies:
        copy.wait_recv()
    total = seen[0].astype(jnp.float32)
    for i in range(1, n):
        total = total + seen[i].astype(jnp.float32)
    out[...] = total
    for copy in copies:
        copy.wait_send()


def share_sum(x, ident):
    n = lax.axis_size("tp")
    dma = pltpu.SemaphoreType.DMA
    return pl.pallas_call(
        functools.partial(share_kernel, n),
        out_shape=jax.ShapeDtypeStruct(x.shape, jnp.float32),
        in_specs=[VM],
        out_specs=VM,
        scratch_shapes=[pltpu.VMEM((n,) + x.shape, x.dtype), dma((n - 1,)), dma((n - 1,)), dma],
        compiler_params=pltpu.CompilerParams(collective_id=ident, has_side_effects=True),
        name="share",
    )(x)


def tp_sum(x, ident, tally=None):
    n = lax.axis_size("tp")
    rows, cols = x.shape
    dma = pltpu.SemaphoreType.DMA
    tallied = tally is not None
    block = pltpu.VMEM((n - 1, rows // n, cols), x.dtype)
    scratch = [block, pltpu.VMEM((rows // n, cols), x.dtype)]
    shape = jax.ShapeDtypeStruct(x.shape, x.dtype)
    if tallied:
        scratch.append(pltpu.VMEM((n,) + tally.shape, jnp.float32))
        shape = (shape, jax.ShapeDtypeStruct(tally.shape, jnp.float32))
    scratch += [dma((n - 1,))] * (6 if tallied else 4) + ([dma] if tallied else [])
    return pl.pallas_call(
        functools.partial(sum_kernel, n, tallied),
        out_shape=shape,
        in_specs=[VM] * (2 if tallied else 1),
        out_specs=(VM, VM) if tallied else VM,
        scratch_shapes=scratch,
        compiler_params=pltpu.CompilerParams(collective_id=ident, has_side_effects=True),
        name="tpsum",
    )(*((x, tally) if tallied else (x,)))


def dots(left, right, dims):
    return lax.dot_general(
        left, right, (dims, ((), ())), precision=HIGH, preferred_element_type=jnp.float32
    )


def scan_parts(x_ref, bc_ref, step_ref, sd_ref, sdt_ref, aux_ref, row_ref):
    length, width = x_ref.shape
    heads = step_ref.shape[1]
    size = width // heads
    states = bc_ref.shape[1] // 2
    order = lambda dim: lax.broadcasted_iota(jnp.int32, (length, length), dim)
    lower = order(0) >= order(1)
    upper = (order(0) <= order(1)).astype(jnp.float32)
    spread = (
        lax.broadcasted_iota(jnp.int32, (heads, width), 1) // size
        == lax.broadcasted_iota(jnp.int32, (heads, width), 0)
    ).astype(jnp.float32)
    rep = lambda v: dots(v, spread, ((1,), (0,)))
    logs = dots(lower.astype(jnp.float32), sd_ref[...], ((1,), (0,)))
    logs_row = dots(sdt_ref[...], upper, ((1,), (0,)))
    aux = aux_ref[...]
    allowed = lower & (aux[:, 0:1] == row_ref[...])
    into = aux[:, 1:2] * jnp.exp(logs)
    tail = jnp.exp(logs[length - 1 : length, :] - logs) * aux[:, 2:3]
    bmat, cmat = bc_ref[:, :states], bc_ref[:, states:]
    scores = dots(cmat, bmat, ((1,), (1,)))

    def weights(h):
        gap = logs[:, h : h + 1] - logs_row[h : h + 1, :]
        return jnp.where(allowed, jnp.exp(jnp.where(allowed, gap, 0.0)), 0.0)

    scaled = x_ref[...] * rep(step_ref[...])
    return heads, size, spread, rep, upper, into, tail, bmat, cmat, scores, weights, scaled


def scan_kernel(x_ref, bc_ref, step_ref, sd_ref, sdt_ref, aux_ref, row_ref, skip_ref, y_ref, made_ref, into_ref):
    heads, size, _, rep, _, into, tail, bmat, _, scores, weights, scaled = scan_parts(
        x_ref, bc_ref, step_ref, sd_ref, sdt_ref, aux_ref, row_ref
    )
    into_ref[...] = into
    made_ref[...] = dots(scaled * rep(tail), bmat, ((0,), (0,))).astype(made_ref.dtype)
    for h in range(heads):
        at = slice(h * size, (h + 1) * size)
        local = dots(weights(h) * scores, scaled[:, at], ((1,), (0,)))
        y_ref[:, at] = local + skip_ref[:, at] * x_ref[:, at]


def back_kernel(
    x_ref, bc_ref, step_ref, sd_ref, sdt_ref, aux_ref, row_ref, skip_ref, decay_ref, dm_ref,
    mixed_ref, enter_ref, leave_ref, dx_ref, dbc_ref, dstep_ref, ddecay_ref, dskip_ref, local_ref,
):
    heads, size, spread, rep, upper, into, tail, bmat, cmat, scores, weights, scaled = scan_parts(
        x_ref, bc_ref, step_ref, sd_ref, sdt_ref, aux_ref, row_ref
    )
    length, states = bmat.shape
    fold = lambda v: dots(v, spread, ((1,), (1,)))
    x, dm = x_ref[...], dm_ref[...]
    enter, leave = enter_ref[...].astype(jnp.float32), leave_ref[...].astype(jnp.float32)
    skip = skip_ref[...]
    tails = rep(tail)
    from_state = tails * dots(bmat, leave, ((1,), (1,)))
    d_scores = jnp.zeros((length, length), jnp.float32)
    for h in range(heads):
        at = slice(h * size, (h + 1) * size)
        weight = weights(h)
        dm_h = dm_ref[:, at]
        d_scores += weight * dots(dm_h, scaled[:, at], ((1,), (1,)))
        local_ref[:, at] = dots(weight * scores, dm_h, ((0,), (0,)))
    d_b = dots(scaled * tails, leave, ((1,), (0,))) + dots(d_scores, cmat, ((0,), (0,)))
    d_c = dots(dm * rep(into), enter, ((1,), (0,))) + dots(d_scores, bmat, ((1,), (0,)))
    dbc_ref[:, :states] = d_b.astype(dbc_ref.dtype)
    dbc_ref[:, states:] = d_c.astype(dbc_ref.dtype)
    d_scaled = local_ref[...] + from_state
    dx_ref[...] = d_scaled * rep(step_ref[...]) + skip * dm
    d_logs = fold(dm * (mixed_ref[...] - skip * x) - scaled * d_scaled)
    ones = jnp.ones((8, states), jnp.float32)
    passed = fold(dots(ones, enter * leave, ((1,), (1,))))[0:1, :]
    last = fold(jnp.sum(scaled * from_state, 0, keepdims=True))
    last = last + into[length - 1 : length, :] * passed
    rest = dots(upper, d_logs, ((1,), (0,))) + last
    dstep_ref[...] = fold(d_scaled * x) + rest * decay_ref[...]
    ddecay_ref[...] = jnp.sum(rest * step_ref[...], 0, keepdims=True)
    dskip_ref[...] = jnp.sum(dm * x, 0, keepdims=True)


def scan_forward(parts):
    length, width = parts[0].shape
    heads, states = parts[2].shape[1], parts[1].shape[1] // 2
    f32 = lambda *shape: jax.ShapeDtypeStruct(shape, jnp.float32)
    return pl.pallas_call(
        scan_kernel,
        out_shape=(
            f32(length, width),
            jax.ShapeDtypeStruct((width, states), jnp.bfloat16),
            f32(length, heads),
        ),
        in_specs=[VM] * len(parts),
        out_specs=(VM,) * 3,
        name="scan_forward",
    )(*parts)


def scan_backward(parts):
    length, width = parts[0].shape
    heads, states = parts[2].shape[1], parts[1].shape[1] // 2
    f32 = lambda *shape: jax.ShapeDtypeStruct(shape, jnp.float32)
    return pl.pallas_call(
        back_kernel,
        out_shape=(
            f32(length, width),
            jax.ShapeDtypeStruct((length, 2 * states), jnp.bfloat16),
            f32(length, heads), f32(1, heads), f32(1, width),
        ),
        in_specs=[VM] * len(parts),
        out_specs=(VM,) * 5,
        scratch_shapes=[pltpu.VMEM((length, width), jnp.float32)],
        name="scan_backward",
    )(*parts)


def body(
    tokens,
    segments,
    cotangent,
    prenorm,
    gate_proj,
    inner_proj,
    state_proj,
    step_proj,
    inner_kernel,
    inner_offset,
    state_kernel,
    state_offset,
    step_bias,
    decay_log,
    skip_gain,
    norm_gain,
    mixer_out,
):
    length = tokens.shape[0]
    model = tokens.shape[1]
    layers = gate_proj.shape[0]
    taps = inner_kernel.shape[1]
    inner_local = gate_proj.shape[2]
    heads_local = step_proj.shape[2]
    head_size = inner_local // heads_local
    state_size = state_proj.shape[2] // 2
    inner_all = inner_local * lax.axis_size("tp")
    feat = model // lax.axis_size("tp")
    feat_start = lax.axis_index("tp") * feat
    start = lax.axis_index("ctx") * length
    seg_pad = jnp.concatenate([jnp.full((taps - 1,), -1, jnp.int32), segments[0]])
    seg_padded = lax.dynamic_slice_in_dim(seg_pad, start, length + taps - 1)
    seg_here = seg_padded[taps - 1 :]
    cont = (seg_padded[taps - 2] == seg_padded[taps - 1]).astype(jnp.float32)
    zeros_state = jnp.zeros((heads_local, head_size, state_size), jnp.float32)
    identity = (jnp.ones((heads_local,), jnp.float32), zeros_state)

    def layer_kernel(layer):
        kernel = jnp.concatenate([inner_kernel[layer], state_kernel[layer]], 1)
        offset = jnp.concatenate([inner_offset[layer], state_offset[layer]])
        return (kernel, offset)

    def split_act(act, layer):
        inner = act[:, :inner_local].reshape(length, heads_local, head_size)
        bmat = act[:, inner_local : inner_local + state_size]
        cmat = act[:, inner_local + state_size :]
        step = jax.nn.softplus(kept_step[layer] + step_bias[layer])
        return (inner, bmat, cmat, step)

    feat_dim = 1
    hidden = tokens.astype(jnp.float32)
    back = cotangent
    kept = []
    kept_step = []
    for layer in range(layers):
        mats = (
            lax.all_gather(gate_proj[layer], ("fsdp", "ctx"), axis=0, tiled=True),
            lax.all_gather(inner_proj[layer], ("fsdp", "ctx"), axis=0, tiled=True),
            lax.all_gather(state_proj[layer], ("fsdp", "ctx"), axis=0, tiled=True),
            lax.all_gather(step_proj[layer], ("fsdp", "ctx"), axis=0, tiled=True),
            lax.all_gather(mixer_out[layer], ("fsdp", "ctx"), axis=0, tiled=True),
        )
        gate_w, inner_w, state_w, step_w, mixer_w = mats
        inverse = None
        normed = rms_apply(hidden, prenorm[layer]).astype(jnp.bfloat16)
        gate = project(normed, gate_w, feat_dim)
        raw = jnp.concatenate(
            [
                project(normed, inner_w, feat_dim).astype(jnp.bfloat16),
                project(normed, state_w, feat_dim).astype(jnp.bfloat16),
            ],
            1,
        )
        step_raw = project(normed, step_w, feat_dim)
        kept_step.append(step_raw)
        before = passed_along(raw[length - (taps - 1) :], "ctx", 1)
        padded = jnp.concatenate([before, raw], 0).astype(jnp.float32)
        kernel, offset = layer_kernel(layer)
        act = conv_apply(padded, seg_padded, kernel, offset)
        inner, bmat, cmat, step = split_act(act, layer)
        decay = -jnp.exp(decay_log[layer])
        partial_mixed, produced = ssd_block(
            inner, bmat, cmat, step, decay, skip_gain[layer], seg_here, cont, zeros_state
        )
        flow = inflow(step, decay, seg_here, cont)
        incoming = prefix((flow[-1], produced), "ctx", link, identity)[1]
        mixed = partial_mixed + jnp.einsum("th,tn,hpn->thp", flow, cmat, incoming, precision=HIGH)
        mixed = mixed.reshape(length, inner_local)
        gated = mixed * jax.nn.silu(gate)
        squares = lax.psum(jnp.sum(gated * gated, 1), "tp")
        scale = lax.rsqrt(squares / inner_all + EPSILON)
        normout = (gated * scale[:, None] * norm_gain[layer]).astype(jnp.bfloat16)
        projected = lax.psum(contract_cols(normout, mixer_w), "tp")
        stored = None
        kept.append(
            (hidden, inverse, stored, normed, gate, padded, incoming, mixed, gated, scale, normout)
        )
        hidden = hidden + projected
    output = hidden
    shard_grads = [None] * layers
    small_grads = [None] * layers
    for layer in reversed(range(layers)):
        hidden_in, inverse, stored, normed, gate, padded, incoming, mixed, gated, scale, normout = (
            kept[layer]
        )
        mats = (
            lax.all_gather(gate_proj[layer], ("fsdp", "ctx"), axis=0, tiled=True),
            lax.all_gather(inner_proj[layer], ("fsdp", "ctx"), axis=0, tiled=True),
            lax.all_gather(state_proj[layer], ("fsdp", "ctx"), axis=0, tiled=True),
            lax.all_gather(step_proj[layer], ("fsdp", "ctx"), axis=0, tiled=True),
            lax.all_gather(mixer_out[layer], ("fsdp", "ctx"), axis=0, tiled=True),
        )
        gate_w, inner_w, state_w, step_w, mixer_w = mats
        gain = norm_gain[layer]
        back_b = back.astype(jnp.bfloat16)
        d_out = project(back_b, mixer_w, feat_dim)
        mixer_grad = grad_rows(back_b, normout, feat_dim)
        norm_grad = jnp.sum(d_out * gated * scale[:, None], 0)
        inner_total = lax.psum(jnp.sum(d_out * gain * gated, 1), "tp")
        d_gated = (
            scale[:, None] * gain * d_out - gated * (scale**3 * inner_total / inner_all)[:, None]
        )
        sigma = jax.nn.sigmoid(gate)
        d_mixed = d_gated * gate * sigma
        d_gate = (d_gated * mixed * sigma * (1.0 + gate * (1.0 - sigma))).astype(jnp.bfloat16)
        kernel, offset = layer_kernel(layer)
        act, conv_pull = jax.vjp(
            lambda pad, ker, off: conv_apply(pad, seg_padded, ker, off), padded, kernel, offset
        )
        inner, bmat, cmat, step = split_act(act, layer)
        decay = -jnp.exp(decay_log[layer])
        flow = inflow(step, decay, seg_here, cont)
        d_mixed3 = d_mixed.reshape(length, heads_local, head_size)
        adjoint = jnp.einsum("th,thp,tn->hpn", flow, d_mixed3, cmat, precision=HIGH)
        carried = entering((flow[-1], adjoint), "ctx", link, identity)[1]

        def mixer_local(inner_v, bmat_v, cmat_v, step_v, decay_v, skip_v, entry):
            part_v, produced_v = ssd_block(
                inner_v, bmat_v, cmat_v, step_v, decay_v, skip_v, seg_here, cont, zeros_state
            )
            flow_v = inflow(step_v, decay_v, seg_here, cont)
            result_v = part_v + jnp.einsum("th,tn,hpn->thp", flow_v, cmat_v, entry, precision=HIGH)
            return (result_v, flow_v[-1][:, None, None] * entry + produced_v)

        _, ssd_pull = jax.vjp(
            mixer_local, inner, bmat, cmat, step, decay, skip_gain[layer], incoming
        )
        g_inner, g_bmat, g_cmat, g_step, g_decay, skip_grad, _ = ssd_pull((d_mixed3, carried))
        g_state = lax.psum(jnp.concatenate([g_bmat, g_cmat], 1).astype(jnp.bfloat16), "tp").astype(
            jnp.float32
        )
        g_act = jnp.concatenate([g_inner.reshape(length, inner_local), g_state], 1)
        g_padded, kernel_grad, offset_grad = conv_pull(g_act)
        returned = passed_along(g_padded[: taps - 1], "ctx", -1)
        g_raw = g_padded[taps - 1 :] + jnp.concatenate(
            [jnp.zeros((length - (taps - 1), g_padded.shape[1]), jnp.float32), returned], 0
        )
        g_step_raw = g_step * jax.nn.sigmoid(kept_step[layer] + step_bias[layer])
        g_inner_b = g_raw[:, :inner_local].astype(jnp.bfloat16)
        g_state_b = g_raw[:, inner_local:].astype(jnp.bfloat16)
        g_step_b = g_step_raw.astype(jnp.bfloat16)
        partial_normed = (
            contract_cols(d_gate, gate_w)
            + contract_cols(g_inner_b, inner_w)
            + contract_cols(g_step_b, step_w)
        )
        d_normed = lax.psum(partial_normed.astype(jnp.bfloat16), "tp").astype(
            jnp.float32
        ) + contract_cols(g_state_b, state_w)
        _, norm_pull = jax.vjp(rms_apply, hidden_in, prenorm[layer])
        d_hidden, prenorm_full = norm_pull(d_normed)
        prenorm_grad = lax.dynamic_slice_in_dim(prenorm_full, feat_start, feat)
        shard_grads[layer] = (
            lax.psum_scatter(
                grad_rows(normed, d_gate, feat_dim),
                ("fsdp", "ctx"),
                scatter_dimension=0,
                tiled=True,
            ),
            lax.psum_scatter(
                grad_rows(normed, g_inner_b, feat_dim),
                ("fsdp", "ctx"),
                scatter_dimension=0,
                tiled=True,
            ),
            lax.psum_scatter(
                grad_rows(normed, g_state_b, feat_dim),
                ("fsdp", "ctx"),
                scatter_dimension=0,
                tiled=True,
            ),
            lax.psum_scatter(
                grad_rows(normed, g_step_b, feat_dim),
                ("fsdp", "ctx"),
                scatter_dimension=0,
                tiled=True,
            ),
            lax.psum_scatter(mixer_grad, ("fsdp", "ctx"), scatter_dimension=0, tiled=True),
        )
        back = back + d_hidden
        small_grads[layer] = (
            prenorm_grad,
            kernel_grad[:, :inner_local],
            offset_grad[:inner_local],
            kernel_grad[:, inner_local:],
            offset_grad[inner_local:],
            jnp.sum(g_step_raw, 0),
            g_decay * decay,
            skip_grad,
            norm_grad,
        )
    output = lax.dynamic_slice_in_dim(output, feat_start, feat, 1)
    back = lax.dynamic_slice_in_dim(back, feat_start, feat, 1)

    def stack_member(groups, member):
        return jnp.stack([groups[layer][member] for layer in range(layers)])

    summed = lax.psum(
        (
            stack_member(small_grads, 0),
            stack_member(small_grads, 1),
            stack_member(small_grads, 2),
            stack_member(small_grads, 3),
            stack_member(small_grads, 4),
            stack_member(small_grads, 5),
            stack_member(small_grads, 6),
            stack_member(small_grads, 7),
            stack_member(small_grads, 8),
        ),
        ("fsdp", "ctx"),
    )
    return (
        output,
        back,
        summed[0],
        stack_member(shard_grads, 0),
        stack_member(shard_grads, 1),
        stack_member(shard_grads, 2),
        stack_member(shard_grads, 3),
        summed[1],
        summed[2],
        summed[3],
        summed[4],
        summed[5],
        summed[6],
        summed[7],
        summed[8],
        stack_member(shard_grads, 4),
    )


def contract_high(left, right, left_dim, right_dim):
    return lax.dot_general(
        left, right, (((left_dim,), (right_dim,)), ((), ())), precision=HIGH
    )


def body_kernels(
    tokens,
    segments,
    cotangent,
    prenorm,
    gate_proj,
    inner_proj,
    state_proj,
    step_proj,
    inner_kernel,
    inner_offset,
    state_kernel,
    state_offset,
    step_bias,
    decay_log,
    skip_gain,
    norm_gain,
    mixer_out,
):
    length = tokens.shape[0]
    model = tokens.shape[1]
    layers = gate_proj.shape[0]
    taps = inner_kernel.shape[1]
    inner_local = gate_proj.shape[2]
    heads_local = step_proj.shape[2]
    head_size = inner_local // heads_local
    state_size = state_proj.shape[2] // 2
    inner_all = inner_local * lax.axis_size("tp")
    feat = model // lax.axis_size("tp")
    feat_start = lax.axis_index("tp") * feat
    start = lax.axis_index("ctx") * length
    seg_pad = jnp.concatenate([jnp.full((taps - 1,), -1, jnp.int32), segments[0]])
    seg_padded = lax.dynamic_slice_in_dim(seg_pad, start, length + taps - 1)
    seg_here = seg_padded[taps - 1 :]
    cont = (seg_padded[taps - 2] == seg_padded[taps - 1]).astype(jnp.float32)
    zeros_state = jnp.zeros((heads_local, head_size, state_size), jnp.float32)
    identity = (jnp.ones((heads_local,), jnp.float32), zeros_state)

    def layer_kernel(layer):
        kernel = jnp.concatenate([inner_kernel[layer], state_kernel[layer]], 1)
        offset = jnp.concatenate([inner_offset[layer], state_offset[layer]])
        return (kernel, offset)

    def split_act(act, layer):
        inner = act[:, :inner_local].reshape(length, heads_local, head_size)
        bmat = act[:, inner_local : inner_local + state_size]
        cmat = act[:, inner_local + state_size :]
        step = jax.nn.softplus(kept_step[layer] + step_bias[layer])
        return (inner, bmat, cmat, step)

    feat_dim = 1
    hidden = tokens.astype(jnp.float32)
    back = cotangent
    kept = []
    kept_step = []
    cols = inner_local
    pad = cols - 2 * state_size - heads_local
    extra = jnp.concatenate(
        [state_proj, step_proj, jnp.zeros(step_proj.shape[:2] + (pad,), step_proj.dtype)], 2
    )
    win, wmix = gather_weights(gate_proj, inner_proj, extra, mixer_out)
    bf = jnp.bfloat16
    fresh = fresh_flags(seg_here, cont)
    aux = jnp.stack(
        [
            seg_here.astype(jnp.float32),
            (jnp.cumsum(fresh) == 0.0).astype(jnp.float32),
            (seg_here == seg_here[-1]).astype(jnp.float32),
        ],
        1,
    )
    seg_row = seg_here.astype(jnp.float32)[None]
    lead = (lax.axis_index("tp") == 0).astype(bf)
    for layer in range(layers):
        inverse = None
        normed = rms_apply(hidden, prenorm[layer]).astype(jnp.bfloat16)
        wide = project(normed, win[layer], feat_dim)
        gate = wide[:, :cols]
        raw = wide[:, cols : 2 * cols + 2 * state_size].astype(bf)
        step_raw = wide[:, 2 * cols + 2 * state_size :][:, :heads_local]
        kept_step.append(step_raw)
        before = passed_along(raw[length - (taps - 1) :], "ctx", 1)
        padded = jnp.concatenate([before, raw], 0).astype(jnp.float32)
        kernel, offset = layer_kernel(layer)
        act = conv_apply(padded, seg_padded, kernel, offset)
        decay = -jnp.exp(decay_log[layer])
        step = jax.nn.softplus(step_raw + step_bias[layer])
        marks = step * decay
        parts = (
            act[:, :inner_local],
            act[:, inner_local:],
            step,
            marks,
            marks.T,
            aux,
            seg_row,
            jnp.repeat(skip_gain[layer], head_size)[None],
        )
        partial_mixed, produced, flow = scan_forward(parts)
        incoming = passed_along(produced, "ctx", 1)
        reach = contract_high(
            act[:, inner_local + state_size :], incoming.astype(jnp.float32), 1, 1
        )
        mixed = partial_mixed + jnp.repeat(flow, head_size, axis=1) * reach
        gated = mixed * jax.nn.silu(gate)
        squares = jnp.broadcast_to(jnp.sum(gated * gated, 1)[None], (8, length))
        lifted = (gated * norm_gain[layer]).astype(bf)
        projected, squares = tp_sum(contract_cols(lifted, wmix[layer]).astype(bf), 3, squares)
        projected = projected.astype(jnp.float32)
        scale = lax.rsqrt(squares[0] / inner_all + EPSILON)
        normout = (gated * scale[:, None] * norm_gain[layer]).astype(bf)
        stored = projected
        kept.append(
            (hidden, (parts, flow, decay), stored, normed, gate, padded, incoming, mixed, gated, scale, normout)
        )
        hidden = hidden + projected * scale[:, None]
    output = hidden
    shard_grads = [None] * layers
    small_grads = [None] * layers
    for layer in reversed(range(layers)):
        hidden_in, inverse, stored, normed, gate, padded, incoming, mixed, gated, scale, normout = (
            kept[layer]
        )
        gain = norm_gain[layer]
        back_b = back.astype(jnp.bfloat16)
        d_out = project(back_b, wmix[layer], feat_dim)
        mixer_grad = grad_rows(back_b, normout, feat_dim)
        norm_grad = jnp.sum(d_out * gated * scale[:, None], 0)
        inner_total = jnp.sum(back_b.astype(jnp.float32) * stored, 1)
        d_gated = (
            scale[:, None] * gain * d_out - gated * (scale**3 * inner_total / inner_all)[:, None]
        )
        sigma = jax.nn.sigmoid(gate)
        d_mixed = d_gated * gate * sigma
        d_gate = (d_gated * mixed * sigma * (1.0 + gate * (1.0 - sigma))).astype(jnp.bfloat16)
        kernel, offset = layer_kernel(layer)
        parts, flow, decay = inverse
        _, conv_pull = jax.vjp(
            lambda pad, ker, off: conv_apply(pad, seg_padded, ker, off), padded, kernel, offset
        )
        cmat = parts[1][:, state_size:]
        adjoint = contract_high(jnp.repeat(flow, head_size, axis=1) * d_mixed, cmat, 0, 0)
        carried = passed_along(adjoint.astype(bf), "ctx", -1)
        g_inner, g_both, g_step, g_decay, skip_grad = scan_backward(
            parts + (decay[None], d_mixed, mixed, incoming, carried)
        )
        g_decay = g_decay[0]
        skip_grad = jnp.sum(skip_grad.reshape(heads_local, head_size), 1)
        g_state = share_sum(g_both, 4)
        g_act = jnp.concatenate([g_inner.reshape(length, inner_local), g_state], 1)
        g_padded, kernel_grad, offset_grad = conv_pull(g_act)
        returned = passed_along(g_padded[: taps - 1], "ctx", -1)
        g_raw = g_padded[taps - 1 :] + jnp.concatenate(
            [jnp.zeros((length - (taps - 1), g_padded.shape[1]), jnp.float32), returned], 0
        )
        g_step_raw = g_step * jax.nn.sigmoid(kept_step[layer] + step_bias[layer])
        g_inner_b = g_raw[:, :inner_local].astype(jnp.bfloat16)
        g_state_b = g_raw[:, inner_local:].astype(jnp.bfloat16)
        g_step_b = g_step_raw.astype(jnp.bfloat16)
        blank = jnp.zeros((length, pad), bf)
        delta = jnp.concatenate([d_gate, g_inner_b, g_state_b, g_step_b, blank], 1)
        single = jnp.concatenate([d_gate, g_inner_b, g_state_b * lead, g_step_b, blank], 1)
        d_normed = tp_sum(contract_cols(single, win[layer]).astype(bf), 5).astype(jnp.float32)
        _, norm_pull = jax.vjp(rms_apply, hidden_in, prenorm[layer])
        d_hidden, prenorm_full = norm_pull(d_normed)
        prenorm_grad = lax.dynamic_slice_in_dim(prenorm_full, feat_start, feat)
        shard_grads[layer] = (
            grad_rows(normed, delta, feat_dim).astype(bf),
            mixer_grad.astype(bf),
        )
        back = back + d_hidden
        small_grads[layer] = (
            prenorm_grad,
            kernel_grad[:, :inner_local],
            offset_grad[:inner_local],
            kernel_grad[:, inner_local:],
            offset_grad[inner_local:],
            jnp.sum(g_step_raw, 0),
            g_decay * decay,
            skip_grad,
            norm_grad,
        )
    output = lax.dynamic_slice_in_dim(output, feat_start, feat, 1)
    back = lax.dynamic_slice_in_dim(back, feat_start, feat, 1)

    def stack_member(groups, member):
        return jnp.stack([groups[layer][member] for layer in range(layers)])

    members = [stack_member(small_grads, member) for member in range(9)]
    flat = jnp.concatenate(
        [
            jnp.pad(m.reshape(-1, m.shape[-1]), ((0, 0), (0, cols - m.shape[-1])))
            for m in members
        ]
    )
    flat = jnp.pad(flat, ((0, -flat.shape[0] % 8), (0, 0)))
    grads = [piece for layer in range(layers) for piece in shard_grads[layer]]
    gate_g, inner_g, state_g, mixer_g, step_g, *summed = reduce_grads(
        grads, flat, [m.shape for m in members], 2 * state_size, heads_local
    )
    return (
        output,
        back,
        summed[0],
        gate_g,
        inner_g,
        state_g,
        step_g,
        summed[1],
        summed[2],
        summed[3],
        summed[4],
        summed[5],
        summed[6],
        summed[7],
        summed[8],
        mixer_g,
    )


def pick(*args):
    nz, ny, n = (lax.axis_size(name) for name in ("fsdp", "ctx", "tp"))
    length, rows, cols = args[0].shape[0], args[4].shape[1], args[4].shape[2]
    heads, states = args[7].shape[2], args[6].shape[2]
    fits = ny == 2 and nz <= 4 and n > 1 and rows % 16 == 0 and cols % 128 == 0
    fits = fits and max(args[3].shape[1] // n, states) <= cols
    fits = fits and length % (16 * n) == 0 and length == SPAN and cols >= states + heads
    return (body_kernels if fits else body)(*args)


def solution(mesh):
    placed = (
        P(("fsdp", "ctx"), None),
        P("fsdp", None),
        P(("fsdp", "ctx"), None),
        P(),
        P(None, ("fsdp", "ctx"), "tp"),
        P(None, ("fsdp", "ctx"), "tp"),
        P(None, ("fsdp", "ctx"), None),
        P(None, ("fsdp", "ctx"), "tp"),
        P(None, None, "tp"),
        P(None, "tp"),
        P(),
        P(),
        P(None, "tp"),
        P(None, "tp"),
        P(None, "tp"),
        P(None, "tp"),
        P(None, ("fsdp", "ctx"), "tp"),
    )
    return jax.shard_map(
        pick,
        mesh=mesh,
        in_specs=placed,
        out_specs=(
            P(("fsdp", "ctx"), "tp"),
            P(("fsdp", "ctx"), "tp"),
            P(None, "tp"),
            P(None, ("fsdp", "ctx"), "tp"),
            P(None, ("fsdp", "ctx"), "tp"),
            P(None, ("fsdp", "ctx"), None),
            P(None, ("fsdp", "ctx"), "tp"),
            P(None, None, "tp"),
            P(None, "tp"),
            P(),
            P(),
            P(None, "tp"),
            P(None, "tp"),
            P(None, "tp"),
            P(None, "tp"),
            P(None, ("fsdp", "ctx"), "tp"),
        ),
        check_vma=False,
    )
```
